256 devices in a mesh: row: 64 (over x, y_lo, z), panel: 4 (over y_hi, core).
Axes of the slice: x: 4, y: 4 (y_hi: 2, y_lo: 2; y = y_hi * 2 + y_lo), z: 8, core: 2. Of those that a mesh axis runs over, the one named last changes fastest.
Arguments:
- pixel_ids: int32 [65536], P('row'), may hold values from 0 to 65535, each once
- quad_offsets: int32 [2, 16, 65536], P(None, None, 'row'), may hold values from 0 to 7
- prior_factor: float32 [65536, 2048], P('row', 'panel'), may hold values from -0.036 to 0.036, as said below
Outputs:
- panel_factor: float32 [65536, 1024], P(('row', 'panel'))
The draws below stay inside these ranges and needn't reach their ends.
Inputs may be any that keep to these rules, and one draw needn't show every extreme that they name: `pixel_ids`: each pixel of the grid appears in exactly one row. `prior_factor`: schur[panel_index] is positive definite.
All inputs are finite; a program needn't handle non-finite values.
Results may differ from the reference program's by a relative error of at most 0.0003.
Values sent between devices are 32-bit elements; how exact they have to be, the bound alone decides.
A program may use at most 128 MiB of HBM per device.

```python
import jax
import jax.numpy as jnp
from jax import lax

Q = 16
B = 1024
ROWS = 65536
QUARTER = 256
PANEL_DEV = 4
K0 = 2048


def draw_prior_factor(key, part):
    values = jnp.clip(jax.random.normal(key, (ROWS, K0), jnp.float32), -4.0, 4.0)
    return values * 0.009


def set_ends(values, stream_key, least, high):
    extent = values.shape
    spot = [jax.random.randint(jax.random.fold_in(stream_key, axis), (), 0, extent[axis]) for axis in range(len(extent))]
    values = values.at[tuple(spot)].set(least)
    longest = extent.index(max(extent))
    spot[longest] = (spot[longest] + 1) % extent[longest]
    return values.at[tuple(spot)].set(high)


def setup_inputs(seed: int = 0) -> dict:
    streams_of = jax.random.split(jax.random.key(seed), 4)
    return {
        "pixel_ids": jax.random.permutation(streams_of[0], ROWS).astype(jnp.int32),
        "quad_offsets": set_ends(jax.random.randint(streams_of[1], (2, Q, ROWS), 0, 8), jax.random.fold_in(streams_of[1], 1), 0, 7).astype(jnp.int32),
        "prior_factor": draw_prior_factor(jax.random.fold_in(streams_of[3], 71), 0),
    }


range_inverse = 1.0

def locate(pixel_ids, quad_offsets):
    column = (pixel_ids % 256).astype(jnp.float32)
    lines = (pixel_ids // 256).astype(jnp.float32)
    east = column[None, :] + (quad_offsets[0].astype(jnp.float32) + 0.5) / 8.0
    north = lines[None, :] + (quad_offsets[1].astype(jnp.float32) + 0.5) / 8.0
    return (east, north)

def cover_tile(east_rows, north_rows, east_cols, north_cols):
    count = east_rows.shape[0]

    def accumulate(index, running):
        east_one = lax.dynamic_index_in_dim(east_rows, index, 0, keepdims=False)
        north_one = lax.dynamic_index_in_dim(north_rows, index, 0, keepdims=False)
        apart_east = east_cols[:, :, None] - east_one[None, None, :]
        apart_north = north_cols[:, :, None] - north_one[None, None, :]
        return running + jnp.sum(jnp.exp(-(apart_east * apart_east + apart_north * apart_north) * range_inverse), axis=0)
    start = jnp.zeros((east_cols.shape[1], east_rows.shape[1]), jnp.float32)
    total = lax.fori_loop(0, count, accumulate, start)
    return total.T / float(count * count)

def reference(pixel_ids, quad_offsets, prior_factor):
    east, north = locate(pixel_ids, quad_offsets)
    column_ids = jnp.arange(B, dtype=jnp.int32)
    panel_index = (column_ids // PANEL_DEV * QUARTER + column_ids % PANEL_DEV).astype(jnp.int32)
    east_panel = east[:, panel_index]
    north_panel = north[:, panel_index]
    prior_panel = prior_factor[panel_index]
    blocks = ROWS // QUARTER

    def one_block(block_id):
        first = (block_id * QUARTER).astype(jnp.int32)
        east_rows = lax.dynamic_slice_in_dim(east, first, QUARTER, 1)
        north_rows = lax.dynamic_slice_in_dim(north, first, QUARTER, 1)
        tile = cover_tile(east_rows, north_rows, east_panel, north_panel)
        row_ids = first + jnp.arange(QUARTER, dtype=jnp.int32)
        tile = tile + jnp.where(row_ids[:, None] == panel_index[None, :], 1.0, 0.0).astype(jnp.float32)
        prior_rows = lax.dynamic_slice_in_dim(prior_factor, first, QUARTER, 0)
        update = jnp.dot(prior_rows.astype(jnp.float32), prior_panel.T.astype(jnp.float32), precision=lax.Precision.HIGHEST, preferred_element_type=jnp.float32)
        return tile - update
    schur = lax.map(one_block, jnp.arange(blocks, dtype=jnp.int32)).reshape(ROWS, B)
    diag_factor = jnp.linalg.cholesky(schur[panel_index])
    return lax.linalg.triangular_solve(diag_factor, schur, left_side=False, lower=True, transpose_a=True)
```

```python
import functools
import math

import jax
import jax.numpy as jnp
from jax import lax
from jax.experimental import pallas as pl
from jax.experimental.pallas import tpu as pltpu
from jax.sharding import PartitionSpec as P

f32, bf16 = jnp.float32, jnp.bfloat16
MESH = pl.DeviceIdType.MESH
NT = (((1,), (1,)), ((), ()))
B = 1024
Q = 16
VMEM_LIMIT = 56 * 2**20
SCALE = -math.log2(math.e) / 64.0


def place():
    row, panel = lax.axis_index("row"), lax.axis_index("panel")
    z = lax.rem(row, 8)
    y = panel // 2 * 2 + lax.rem(row // 8, 2)
    return row // 16, y, z, lax.rem(panel, 2)


def device(x, y, z, core):
    return {"row": (x * 2 + lax.rem(y, 2)) * 8 + z, "panel": y // 2 * 2 + core}


def meet(partners):
    barrier = pltpu.get_barrier_semaphore()
    for partner in partners:
        pl.semaphore_signal(barrier, inc=1, device_id=partner, device_id_type=MESH)
    pl.semaphore_wait(barrier, len(partners))


def send(src, dst, send_sem, recv_sem, target):
    return pltpu.make_async_remote_copy(
        src_ref=src, dst_ref=dst, send_sem=send_sem, recv_sem=recv_sem,
        device_id=target, device_id_type=MESH,
    )


def points_kernel(own, every, here, sz, rz, sb, rb):
    row, panel = lax.axis_index("row"), lax.axis_index("panel")
    z, base = lax.rem(row, 8), row // 8
    along = [{"row": base * 8 + lax.rem(z + d, 8), "panel": panel} for d in range(1, 8)]
    across = [{"row": lax.rem(base + d, 8) * 8 + z, "panel": panel} for d in range(1, 8)]
    meet(along + across)
    local = pltpu.make_async_copy(own, every.at[row], here)
    local.start()
    first = [send(own, every.at[row], sz.at[d], rz.at[d], along[d]) for d in range(7)]
    for copy in first:
        copy.start()
    local.wait()
    for copy in first:
        copy.wait_recv()
    slab = every.at[pl.ds(base * 8, 8)]
    second = [send(slab, slab, sb.at[d], rb.at[d], across[d]) for d in range(7)]
    for copy in second:
        copy.start()
    for copy in second:
        copy.wait_recv()
    for copy in first + second:
        copy.wait_send()


def gather_points(own):
    return pl.pallas_call(
        points_kernel,
        out_shape=jax.ShapeDtypeStruct((64, 8, 128), f32),
        in_specs=[pl.BlockSpec(memory_space=pl.ANY)],
        out_specs=pl.BlockSpec(memory_space=pl.ANY),
        scratch_shapes=[pltpu.SemaphoreType.DMA] + [pltpu.SemaphoreType.DMA((7,))] * 4,
        compiler_params=pltpu.CompilerParams(collective_id=0, has_side_effects=True),
    )(own)


def gather_kernel(own, prior, every, mine, here, s1, r1, s2, r2, s3, r3, s4, r4, sq, rq):
    x, y, z, core = place()
    row, panel = lax.axis_index("row"), lax.axis_index("panel")
    other = 1 - core

    def at(dx, dy):
        return lax.rem(x + dx, 4), lax.rem(y + dy, 4)

    def middle(i):
        cx, cy = at(core * i, other * i)
        return device(cx, cy, z, core)

    def last(i):
        cx, cy = at(other * i, core * i)
        return device(cx, cy, z, core)

    along = [device(x, y, lax.rem(z + d, 8), core) for d in range(1, 8)]
    twin = device(x, y, z, other)
    quarters = [{"row": row, "panel": lax.rem(panel + d, 4)} for d in range(1, 4)]
    far = device(x, lax.rem(y + 2, 4), z, other)
    meet(along + [middle(i) for i in range(1, 4)] + [last(i) for i in range(1, 4)] + [twin, far])

    locals_ = [
        pltpu.make_async_copy(own, every.at[panel, row], here.at[0]),
        pltpu.make_async_copy(prior.at[pl.ds(panel * 256, 256)], mine.at[panel], here.at[1]),
    ]
    for copy in locals_:
        copy.start()
    first = [send(own, every.at[panel, row], s1.at[d], r1.at[d], along[d]) for d in range(7)]
    for copy in first:
        copy.start()
    swaps = []
    for d in range(3):
        to = lax.rem(panel + d + 1, 4)
        swaps.append(send(prior.at[pl.ds(to * 256, 256)], mine.at[panel], sq.at[d], rq.at[d], quarters[d]))

    def slab(k, i):
        cx, cy = at(core * (4 - k) + other * (4 - i), core * (4 - i) + other * (4 - k))
        return every.at[cy // 2 * 2 + core, pl.ds((cx * 2 + lax.rem(cy, 2)) * 8, 8)]

    sent = list(first) + swaps

    def hand(k, i):
        copy = send(slab(k, i), slab(k, i), s4.at[k, i], r4.at[k, i], twin)
        copy.start()
        sent.append(copy)

    def onward(k):
        copies = [send(slab(k, 0), slab(k, 0), s3.at[k, i - 1], r3.at[k, i - 1], last(i)) for i in range(1, 4)]
        for copy in copies:
            copy.start()
        sent.extend(copies)
        return copies

    for copy in locals_:
        copy.wait()
    for copy in first:
        copy.wait_recv()
    second = [send(slab(0, 0), slab(0, 0), s2.at[i - 1], r2.at[i - 1], middle(i)) for i in range(1, 4)]
    for copy in second:
        copy.start()
    sent.extend(second)
    third = [onward(0)]
    hand(0, 0)
    for k in range(1, 4):
        second[k - 1].wait_recv()
        third.append(onward(k))
        hand(k, 0)
    for copy in swaps:
        copy.start()
    for k in range(4):
        for i in range(1, 4):
            third[k][i - 1].wait_recv()
            hand(k, i)
    for k in range(4):
        for i in range(4):
            send(slab(k, i), slab(k, i), s4.at[k, i], r4.at[k, i], twin).wait_recv()
    for copy in swaps:
        copy.wait_recv()
    for copy in sent:
        copy.wait_send()


def gather(own, prior):
    dma = pltpu.SemaphoreType.DMA
    width = own.shape[1]
    return pl.pallas_call(
        gather_kernel,
        out_shape=[
            jax.ShapeDtypeStruct((4, 64, 16, width), f32),
            jax.ShapeDtypeStruct((4, 256, 512), f32),
        ],
        in_specs=[pl.BlockSpec(memory_space=pl.ANY)] * 2,
        out_specs=[pl.BlockSpec(memory_space=pl.ANY)] * 2,
        scratch_shapes=[
            dma((2,)), dma((7,)), dma((7,)), dma((3,)), dma((3,)),
            dma((4, 3)), dma((4, 3)), dma((4, 4)), dma((4, 4)), dma((3,)), dma((3,)),
        ],
        compiler_params=pltpu.CompilerParams(collective_id=1, has_side_effects=True),
    )(own, prior)


def cover_kernel(er, nr, ec, nc, out):
    width = 256

    def rows(i, _):
        rs = pl.ds(pl.multiple_of(i * 8, 8), 8)
        e8, n8 = er[rs, :], nr[rs, :]
        e = [jnp.broadcast_to(e8[:, a : a + 1], (8, width)) for a in range(Q)]
        n = [jnp.broadcast_to(n8[:, a : a + 1], (8, width)) for a in range(Q)]

        def cols(j, _):
            cs = pl.ds(pl.multiple_of(j * width, width), width)
            acc = [jnp.zeros((8, width), f32) for _ in range(4)]
            for b in range(Q):
                eb = jnp.broadcast_to(ec[b : b + 1, cs], (8, width))
                nb = jnp.broadcast_to(nc[b : b + 1, cs], (8, width))
                for a in range(Q):
                    de, dn = e[a] - eb, n[a] - nb
                    acc[a % 4] = acc[a % 4] + jnp.exp2((de * de + dn * dn) * SCALE)
            out[rs, cs] = ((acc[0] + acc[1]) + (acc[2] + acc[3])) * (1.0 / (Q * Q))
            return 0

        lax.fori_loop(0, ec.shape[1] // width, cols, 0)
        return 0

    lax.fori_loop(0, er.shape[0] // 8, rows, 0)


def cover(er, nr, ec, nc):
    shape = (er.shape[0], ec.shape[1])
    return pl.pallas_call(
        cover_kernel,
        out_shape=jax.ShapeDtypeStruct(shape, f32),
        in_specs=[pl.BlockSpec(memory_space=pltpu.VMEM)] * 4,
        out_specs=pl.BlockSpec(memory_space=pltpu.VMEM),
        compiler_params=pltpu.CompilerParams(vmem_limit_bytes=VMEM_LIMIT),
    )(er, nr, ec, nc)


def split(v):
    hi = v.astype(bf16)
    return hi, (v - hi.astype(f32)).astype(bf16)


def dot3(ah, al, bh, bl):
    dot = functools.partial(lax.dot_general, dimension_numbers=NT, preferred_element_type=f32)
    return dot(ah, bh) + (dot(ah, bl) + dot(al, bh))


def factor_inverse(block):
    sub = lax.broadcasted_iota(jnp.int32, (8, 128), 0)
    lane = lax.broadcasted_iota(jnp.int32, (8, 128), 1)
    rest = [block[8 * s : 8 * s + 8, :] for s in range(16)]
    unit = [jnp.where(lane == sub + 8 * s, 1.0, 0.0).astype(f32) for s in range(16)]

    def down(v, k):
        return jnp.broadcast_to(v[k : k + 1, :], (8, 128))

    def across(v, k):
        return jnp.broadcast_to(v[:, k : k + 1], (8, 128))

    out = []
    for s in range(16):
        strip, other = rest[s], unit[s]
        cols = [across(strip, 8 * s + k) for k in range(8)]
        final = jnp.zeros((8, 128), f32)
        for k in range(8):
            pivot_row = sub == k
            pivot = down(cols[k], k)
            inverse = 1.0 / pivot
            scale = jnp.where(pivot_row, -inverse, cols[k] * inverse)

            def step(v):
                return jnp.where(pivot_row, 0.0, v) - scale * down(v, k)

            final = jnp.where(pivot_row, other * lax.rsqrt(pivot), final)
            strip, other = step(strip), step(other)
            for j in range(k + 1, 8):
                cols[j] = step(cols[j])
        out.append(final)
        for t in range(s + 1, 16):
            a, b = rest[t], unit[t]
            for k in range(8):
                c = across(rest[t], 8 * s + k)
                a = a - c * down(strip, k)
                b = b - c * down(other, k)
            rest[t], unit[t] = a, b
    return jnp.concatenate(out, axis=0)


def solve_kernel(every, mine, own_cover, out, ph, pl_, m, lh, ll, column):
    row, panel = lax.axis_index("row"), lax.axis_index("panel")
    first = (row * 4 + panel) * 4

    def halves(c, _):
        rc = pl.ds(pl.multiple_of(c * 256, 256), 256)
        for p in range(4):
            ph[p, rc, :], pl_[p, rc, :] = split(every[p, rc, 0:512])
        return 0

    lax.fori_loop(0, 4, halves, 0)
    for p in range(4):
        ph[p, 1024:1280, :], pl_[p, 1024:1280, :] = split(mine[p])
    ids = lax.broadcasted_iota(jnp.int32, (256, 256), 0)
    col = lax.broadcasted_iota(jnp.int32, (256, 256), 1)
    unit = jnp.where(ids == col, 1.0, 0.0).astype(f32)
    for j in range(4):
        cj = slice(j * 256, j * 256 + 256)
        own = jnp.where((ids < 4) & (col + j * 256 == first + ids), 1.0, 0.0).astype(f32)
        m[1024:1280, cj] = own_cover[:, cj] + own
        m[cj, cj] = every[j, cj, 512:768] + unit
        for i in range(j + 1, 4):
            ci = slice(i * 256, i * 256 + 256)
            m[ci, cj] = every[j, ci, 512:768]

    def update(j, _):
        cj = pl.ds(pl.multiple_of(j * 256, 256), 256)

        def block(i, _):
            ci = pl.ds(pl.multiple_of(i * 256, 256), 256)
            acc = m[ci, cj]
            for p in range(4):
                acc = acc - dot3(ph[p, ci, :], pl_[p, ci, :], ph[p, cj, :], pl_[p, cj, :])
            m[ci, cj] = acc
            return 0

        lax.fori_loop(j, 5, block, 0)
        return 0

    lax.fori_loop(0, 4, update, 0)

    def one(k, _):
        ck = pl.ds(pl.multiple_of(k * 128, 128), 128)

        def left(c, _):
            rc = pl.ds(pl.multiple_of(c * 256, 256), 256)

            def term(j, acc):
                cj = pl.ds(pl.multiple_of(j * 128, 128), 128)
                return acc - dot3(lh[rc, cj], ll[rc, cj], lh[ck, cj], ll[ck, cj])

            column[rc, :] = lax.fori_loop(0, k, term, m[rc, ck])
            return 0

        lax.fori_loop(k // 2, 5, left, 0)
        ih, il = split(factor_inverse(column[ck, :]))

        def right(c, _):
            rc = pl.ds(pl.multiple_of(c * 256, 256), 256)
            rh, rl = split(column[rc, :])
            v = dot3(rh, rl, ih, il)
            lh[rc, ck], ll[rc, ck] = split(v)

            @pl.when(c == 4)
            def _():
                out[:, ck] = v

            return 0

        lax.fori_loop(k // 2, 5, right, 0)
        return 0

    lax.fori_loop(0, 8, one, 0)


def solve(every, mine, own_cover):
    return pl.pallas_call(
        solve_kernel,
        out_shape=jax.ShapeDtypeStruct((256, B), f32),
        in_specs=[pl.BlockSpec(memory_space=pltpu.VMEM)] * 3,
        out_specs=pl.BlockSpec(memory_space=pltpu.VMEM),
        scratch_shapes=[
            pltpu.VMEM((4, 1280, 512), bf16), pltpu.VMEM((4, 1280, 512), bf16),
            pltpu.VMEM((1280, B), f32),
            pltpu.VMEM((1280, B), bf16), pltpu.VMEM((1280, B), bf16),
            pltpu.VMEM((1280, 128), f32),
        ],
        compiler_params=pltpu.CompilerParams(vmem_limit_bytes=VMEM_LIMIT),
    )(every, mine, own_cover)


def local(pixel_ids, quad_offsets, prior_factor):
    panel = lax.axis_index("panel")
    cell = jnp.stack([pixel_ids % 256, pixel_ids // 256])
    points = (cell[:, None, :] * 8 + quad_offsets).astype(f32)
    quarters = points.reshape(2, Q, 4, 256)[:, :, :, :4].reshape(2, Q, 16)
    packed = jnp.concatenate([quarters.reshape(4, 128), jnp.zeros((4, 128), f32)])
    got = gather_points(packed)
    cols = got[:, :4].reshape(64, 2, Q, 16).transpose(1, 2, 0, 3).reshape(2, Q, B)
    own_rows = lax.dynamic_slice_in_dim(points, panel * 256, 256, 2).transpose(0, 2, 1)
    own_cover = cover(own_rows[0], own_rows[1], cols[0], cols[1])
    some_cols = lax.dynamic_slice_in_dim(cols, panel * 256, 256, 2)
    some_rows = quarters.transpose(0, 2, 1)
    some_cover = cover(some_rows[0], some_rows[1], some_cols[0], some_cols[1])
    panel_rows = prior_factor.reshape(4, 256, 512)[:, :4].reshape(16, 512)
    every, mine = gather(jnp.concatenate([panel_rows, some_cover], axis=1), prior_factor)
    return solve(every.reshape(4, B, 768), mine, own_cover)


def solution(mesh):
    return jax.shard_map(
        local,
        mesh=mesh,
        in_specs=(P("row"), P(None, None, "row"), P("row", "panel")),
        out_specs=P(("row", "panel"), None),
        check_vma=False,
    )
```

```python
import functools
import math

import jax
import jax.numpy as jnp
from jax import lax
from jax.experimental import pallas as pl
from jax.experimental.pallas import tpu as pltpu
from jax.sharding import PartitionSpec as P

f32, bf16 = jnp.float32, jnp.bfloat16
MESH = pl.DeviceIdType.MESH
NT = (((1,), (1,)), ((), ()))
B = 1024
Q = 16
VMEM_LIMIT = 56 * 2**20
SCALE = -math.log2(math.e) / 64.0


def place():
    row, panel = lax.axis_index("row"), lax.axis_index("panel")
    z = lax.rem(row, 8)
    y = panel // 2 * 2 + lax.rem(row // 8, 2)
    return row // 16, y, z, lax.rem(panel, 2)


def device(x, y, z, core):
    return {"row": (x * 2 + lax.rem(y, 2)) * 8 + z, "panel": y // 2 * 2 + core}


def meet(partners):
    barrier = pltpu.get_barrier_semaphore()
    for partner in partners:
        pl.semaphore_signal(barrier, inc=1, device_id=partner, device_id_type=MESH)
    pl.semaphore_wait(barrier, len(partners))


def send(src, dst, send_sem, recv_sem, target):
    return pltpu.make_async_remote_copy(
        src_ref=src, dst_ref=dst, send_sem=send_sem, recv_sem=recv_sem,
        device_id=target, device_id_type=MESH,
    )


class Ring:
    names = ("sz", "rz", "s2", "r2", "t2", "u2", "s3", "r3", "t3", "u3", "s4", "r4")
    sizes = ((7,), (7,), (2,), (2,), (2,), (2,), (4, 2), (4, 2), (4, 2), (4, 2), (4, 4), (4, 4))

    def __init__(self, own, every, sems):
        self.own, self.every, self.sem = own, every, dict(zip(self.names, sems))
        self.x, self.y, self.z, self.core = place()
        self.row, self.panel = lax.axis_index("row"), lax.axis_index("panel")

    def slab(self, k, i, part=None):
        core, other = self.core, 1 - self.core
        cx = lax.rem(self.x + core * (4 - k) + other * (4 - i), 4)
        cy = lax.rem(self.y + core * (4 - i) + other * (4 - k), 4)
        start = (cx * 2 + lax.rem(cy, 2)) * 8
        blocks = pl.ds(start, 8) if part is None else pl.ds(start + 4 * part, 4)
        return self.every.at[cy // 2 * 2 + core, blocks]

    def neighbour(self, dim, way):
        step = 1 + 2 * way
        along_y = (1 - self.core) if dim == 0 else self.core
        cx = lax.rem(self.x + step * (1 - along_y), 4)
        cy = lax.rem(self.y + step * along_y, 4)
        return device(cx, cy, self.z, self.core)

    def z_copies(self):
        to = [device(self.x, self.y, lax.rem(self.z + d, 8), self.core) for d in range(1, 8)]
        slot = self.every.at[self.panel, self.row]
        return [send(self.own, slot, self.sem["sz"].at[d], self.sem["rz"].at[d], to[d]) for d in range(7)]

    def middle(self):
        part = self.slab(0, 0)
        return [send(part, part, self.sem["s2"].at[w], self.sem["r2"].at[w], self.neighbour(0, w)) for w in range(2)]

    def middle_far(self):
        parts = [self.slab(1, 0, 0), self.slab(3, 0, 1)]
        return [send(parts[w], parts[w], self.sem["t2"].at[w], self.sem["u2"].at[w], self.neighbour(0, w)) for w in range(2)]

    def last(self, k):
        part = self.slab(k, 0)
        return [send(part, part, self.sem["s3"].at[k, w], self.sem["r3"].at[k, w], self.neighbour(1, w)) for w in range(2)]

    def last_far(self, k):
        parts = [self.slab(k, 1, 0), self.slab(k, 3, 1)]
        return [send(parts[w], parts[w], self.sem["t3"].at[k, w], self.sem["u3"].at[k, w], self.neighbour(1, w)) for w in range(2)]

    def hand(self, k, i):
        part = self.slab(k, i)
        twin = device(self.x, self.y, self.z, 1 - self.core)
        return [send(part, part, self.sem["s4"].at[k, i], self.sem["r4"].at[k, i], twin)]

    def all(self):
        copies = self.z_copies() + self.middle() + self.middle_far()
        for k in range(4):
            copies += self.last(k) + self.last_far(k)
        return copies + [c for k in range(4) for i in range(4) for c in self.hand(k, i)]


def begin(*groups):
    for copies in groups:
        for copy in copies:
            copy.start()


def arrive(*groups):
    for copies in groups:
        for copy in copies:
            copy.wait_recv()


def cover_rows(er, nr, cols, first_tile, tiles, out, i):
    rs = pl.ds(pl.multiple_of(i * 8, 8), 8)
    e8, n8 = er[rs, :], nr[rs, :]
    e = [jnp.broadcast_to(e8[:, a : a + 1], (8, 128)) for a in range(Q)]
    n = [jnp.broadcast_to(n8[:, a : a + 1], (8, 128)) for a in range(Q)]

    def pair(j, _):
        for half in range(2):
            t = 2 * j + half
            acc = [jnp.zeros((8, 128), f32) for _ in range(4)]
            for b in range(Q):
                eb = jnp.broadcast_to(cols[first_tile + t, b : b + 1, :], (8, 128))
                nb = jnp.broadcast_to(cols[first_tile + t, Q + b : Q + b + 1, :], (8, 128))
                for a in range(Q):
                    de, dn = e[a] - eb, n[a] - nb
                    acc[a % 4] = acc[a % 4] + jnp.exp2((de * de + dn * dn) * SCALE)
            cs = pl.ds(pl.multiple_of(t * 128, 128), 128)
            out[rs, cs] = ((acc[0] + acc[1]) + (acc[2] + acc[3])) * (1.0 / (Q * Q))
        return 0

    lax.fori_loop(0, tiles // 2, pair, 0)


def gather_kernel(own, prior, pts, er, nr, se, sn, pe, ce, mine, cover, some, zpts, cols, relay, *sems):
    x, y, z, core = place()
    row, panel = lax.axis_index("row"), lax.axis_index("panel")
    count = len(Ring.names)
    here, psz, prz, ps, pr, qs, qr, qs2, qr2, ts, tr = sems[2 * count :]
    base = row // 8
    y1, ahead, back = y // 2 * 2 + 1 - lax.rem(y, 2), lax.rem(y + 1, 4), lax.rem(y + 3, 4)
    twin = device(x, y, z, 1 - core)
    along = [device(x, y, lax.rem(z + d, 8), core) for d in range(1, 8)]
    meet(
        along
        + [device(lax.rem(x + d, 4), y, z, core) for d in range(1, 4)]
        + [device(lax.rem(x + d, 4), y1, z, core) for d in range(1, 4)]
        + [device(x, ahead, z, core), device(x, back, z, core)]
        + [device(x, ahead, z, 1 - core), device(x, back, z, 1 - core), twin]
    )
    points = [send(pts, zpts.at[d], psz.at[d], prz.at[d], along[d]) for d in range(7)]
    begin(points)
    prior_ring = Ring(own, pe, sems[:count])
    cover_ring = Ring(some, ce, sems[count : 2 * count])
    local_prior = pltpu.make_async_copy(own, pe.at[panel, row], here.at[0])
    local_mine = pltpu.make_async_copy(prior.at[pl.ds(panel * 256, 256)], mine.at[panel], here.at[1])
    local_prior.start()
    local_mine.start()
    begin(prior_ring.z_copies())
    arrive(points)
    total = pts[...]
    for d in range(7):
        total = total + zpts[d]
    cols[base] = total
    spread = [
        send(cols.at[base], cols.at[base], ps.at[d], pr.at[d],
             {"row": lax.rem(base + d + 1, 8) * 8 + z, "panel": panel})
        for d in range(7)
    ]
    begin(spread)
    arrive(spread)
    for i in range(2):
        cover_rows(se, sn, cols, panel * 2, 2, some, i)
    local_cover = pltpu.make_async_copy(some, ce.at[panel, row], here.at[2])
    local_cover.start()
    begin(cover_ring.z_copies())

    def exchange():
        first, second, landing = [], [], []
        for w in range(2):
            to = (ahead, back)[w]
            source = (back, ahead)[w] // 2 * 2 + core
            for c in range(2):
                rows = (1 - y // 2) * 512 + c * 256 + w * 128
                first.append(send(prior.at[pl.ds(rows, 128)], relay.at[w, c], qs.at[w, c], qr.at[w, c],
                                  device(x, to, z, core)))
                hop = functools.partial(send, relay.at[w, c], mine.at[source, pl.ds(w * 128, 128)], qs2.at[w, c])
                second.append(hop(qr2.at[w, core], device(x, to, z, c)))
                landing.append(hop(qr2.at[w, c], device(x, to, z, c)))
        rows = (y // 2 * 2 + 1 - core) * 256
        return first, second, landing, [send(prior.at[pl.ds(rows, 256)], mine.at[panel], ts, tr, twin)]

    def start_ring(ring, local):
        local.wait()
        arrive(ring.z_copies())
        begin(ring.middle(), ring.last(0), ring.hand(0, 0))

    def middle_in(ring):
        arrive(ring.middle())
        begin(ring.middle_far(), ring.last(1), ring.last(3), ring.hand(1, 0), ring.hand(3, 0))

    def middle_far_in(ring):
        arrive(ring.middle_far())
        begin(ring.last(2), ring.hand(2, 0))

    def last_in(ring, k):
        arrive(ring.last(k))
        begin(ring.last_far(k), ring.hand(k, 1), ring.hand(k, 3))

    def last_far_in(ring):
        for k in range(4):
            arrive(ring.last_far(k))
            begin(ring.hand(k, 2))

    def at0():
        start_ring(prior_ring, local_prior)
        first, _, _, near = exchange()
        begin(first, near)

    def at1():
        middle_in(prior_ring)

    def at2():
        start_ring(cover_ring, local_cover)

    def at3():
        middle_far_in(prior_ring)
        middle_in(cover_ring)

    def at5():
        middle_far_in(cover_ring)
        first, second, _, _ = exchange()
        arrive(first)
        begin(second)

    def at8():
        last_in(prior_ring, 0)

    def at10():
        last_in(prior_ring, 1)
        last_in(prior_ring, 3)

    def at12():
        last_in(prior_ring, 2)
        last_in(cover_ring, 0)

    def at14():
        last_in(cover_ring, 1)
        last_in(cover_ring, 3)

    def at16():
        last_in(cover_ring, 2)

    def at18():
        last_far_in(prior_ring)

    def at20():
        last_far_in(cover_ring)

    steps = {0: at0, 1: at1, 2: at2, 3: at3, 5: at5, 8: at8, 10: at10, 12: at12, 14: at14, 16: at16, 18: at18, 20: at20}

    def rows(i, _):
        for when, step in steps.items():
            pl.when(i == when)(step)
        cover_rows(er, nr, cols, 0, 8, cover, i)
        return 0

    lax.fori_loop(0, 32, rows, 0)
    first, second, landing, near = exchange()
    for ring in (prior_ring, cover_ring):
        for k in range(4):
            for i in range(4):
                arrive(ring.hand(k, i))
    arrive(landing, near)
    local_mine.wait()
    for copy in points + spread + prior_ring.all() + cover_ring.all() + first + second + near:
        copy.wait_send()


def gather(own, prior, pts, er, nr, se, sn):
    dma = pltpu.SemaphoreType.DMA
    hbm, vmem = pl.BlockSpec(memory_space=pl.ANY), pl.BlockSpec(memory_space=pltpu.VMEM)
    ring = [dma(size) for size in Ring.sizes]
    return pl.pallas_call(
        gather_kernel,
        out_shape=[
            jax.ShapeDtypeStruct((4, 64, 16, 512), f32),
            jax.ShapeDtypeStruct((4, 64, 16, 256), f32),
            jax.ShapeDtypeStruct((4, 256, 512), f32),
            jax.ShapeDtypeStruct((256, B), f32),
        ],
        in_specs=[hbm, hbm, vmem, vmem, vmem, vmem, vmem],
        out_specs=[hbm, hbm, hbm, vmem],
        scratch_shapes=[
            pltpu.VMEM((16, 256), f32), pltpu.VMEM((7, 32, 128), f32), pltpu.VMEM((8, 32, 128), f32),
            pltpu.VMEM((2, 2, 128, 512), f32),
            *ring, *ring, dma((3,)), dma((7,)), dma((7,)), dma((7,)), dma((7,)),
            dma((2, 2)), dma((2, 2)), dma((2, 2)), dma((2, 2)), dma, dma,
        ],
        compiler_params=pltpu.CompilerParams(
            collective_id=0, has_side_effects=True, vmem_limit_bytes=VMEM_LIMIT
        ),
    )(own, prior, pts, er, nr, se, sn)


def split(v):
    hi = v.astype(bf16)
    return hi, (v - hi.astype(f32)).astype(bf16)


def dot3(ah, al, bh, bl):
    dot = functools.partial(lax.dot_general, dimension_numbers=NT, preferred_element_type=f32)
    return dot(ah, bh) + (dot(ah, bl) + dot(al, bh))


def factor_inverse(block):
    sub = lax.broadcasted_iota(jnp.int32, (8, 128), 0)
    lane = lax.broadcasted_iota(jnp.int32, (8, 128), 1)
    rest = [block[8 * s : 8 * s + 8, :] for s in range(16)]
    unit = [jnp.where(lane == sub + 8 * s, 1.0, 0.0).astype(f32) for s in range(16)]

    def down(v, k):
        return jnp.broadcast_to(v[k : k + 1, :], (8, 128))

    def across(v, k):
        return jnp.broadcast_to(v[:, k : k + 1], (8, 128))

    out = []
    for s in range(16):
        strip, other = rest[s], unit[s]
        cols = [across(strip, 8 * s + k) for k in range(8)]
        final = jnp.zeros((8, 128), f32)
        for k in range(8):
            pivot_row = sub == k
            pivot = down(cols[k], k)
            inverse = 1.0 / pivot
            scale = jnp.where(pivot_row, -inverse, cols[k] * inverse)

            def step(v):
                return jnp.where(pivot_row, 0.0, v) - scale * down(v, k)

            final = jnp.where(pivot_row, other * lax.rsqrt(pivot), final)
            strip, other = step(strip), step(other)
            for j in range(k + 1, 8):
                cols[j] = step(cols[j])
        out.append(final)
        for t in range(s + 1, 16):
            a, b = rest[t], unit[t]
            for k in range(8):
                c = across(rest[t], 8 * s + k)
                a = a - c * down(strip, k)
                b = b - c * down(other, k)
            rest[t], unit[t] = a, b
    return jnp.concatenate(out, axis=0)


def solve_kernel(every, panel_cover, mine, own_cover, out, ph, pl_, m, lh, ll, column):
    row, panel = lax.axis_index("row"), lax.axis_index("panel")
    first = (row * 4 + panel) * 4

    def halves(c, _):
        rc = pl.ds(pl.multiple_of(c * 256, 256), 256)
        for p in range(4):
            ph[p, rc, :], pl_[p, rc, :] = split(every[p, rc, :])
        return 0

    lax.fori_loop(0, 4, halves, 0)
    for p in range(4):
        ph[p, 1024:1280, :], pl_[p, 1024:1280, :] = split(mine[p])
    ids = lax.broadcasted_iota(jnp.int32, (256, 256), 0)
    col = lax.broadcasted_iota(jnp.int32, (256, 256), 1)
    unit = jnp.where(ids == col, 1.0, 0.0).astype(f32)
    for j in range(4):
        cj = slice(j * 256, j * 256 + 256)
        own = jnp.where((ids < 4) & (col + j * 256 == first + ids), 1.0, 0.0).astype(f32)
        m[1024:1280, cj] = own_cover[:, cj] + own
        m[cj, cj] = panel_cover[j, cj, :] + unit
        for i in range(j + 1, 4):
            ci = slice(i * 256, i * 256 + 256)
            m[ci, cj] = panel_cover[j, ci, :]

    def update(j, _):
        cj = pl.ds(pl.multiple_of(j * 256, 256), 256)

        def block(i, _):
            ci = pl.ds(pl.multiple_of(i * 256, 256), 256)
            acc = m[ci, cj]
            for p in range(4):
                acc = acc - dot3(ph[p, ci, :], pl_[p, ci, :], ph[p, cj, :], pl_[p, cj, :])
            m[ci, cj] = acc
            return 0

        lax.fori_loop(j, 5, block, 0)
        return 0

    lax.fori_loop(0, 4, update, 0)

    def one(k, _):
        ck = pl.ds(pl.multiple_of(k * 128, 128), 128)

        def left(c, _):
            rc = pl.ds(pl.multiple_of(c * 256, 256), 256)

            def term(j, acc):
                cj = pl.ds(pl.multiple_of(j * 128, 128), 128)
                return acc - dot3(lh[rc, cj], ll[rc, cj], lh[ck, cj], ll[ck, cj])

            column[rc, :] = lax.fori_loop(0, k, term, m[rc, ck])
            return 0

        lax.fori_loop(k // 2, 5, left, 0)
        ih, il = split(factor_inverse(column[ck, :]))

        def right(c, _):
            rc = pl.ds(pl.multiple_of(c * 256, 256), 256)
            rh, rl = split(column[rc, :])
            v = dot3(rh, rl, ih, il)
            lh[rc, ck], ll[rc, ck] = split(v)

            @pl.when(c == 4)
            def _():
                out[:, ck] = v

            return 0

        lax.fori_loop(k // 2, 5, right, 0)
        return 0

    lax.fori_loop(0, 8, one, 0)


def solve(every, panel_cover, mine, own_cover):
    return pl.pallas_call(
        solve_kernel,
        out_shape=jax.ShapeDtypeStruct((256, B), f32),
        in_specs=[pl.BlockSpec(memory_space=pltpu.VMEM)] * 4,
        out_specs=pl.BlockSpec(memory_space=pltpu.VMEM),
        scratch_shapes=[
            pltpu.VMEM((4, 1280, 512), bf16), pltpu.VMEM((4, 1280, 512), bf16),
            pltpu.VMEM((1280, B), f32),
            pltpu.VMEM((1280, B), bf16), pltpu.VMEM((1280, B), bf16),
            pltpu.VMEM((1280, 128), f32),
        ],
        compiler_params=pltpu.CompilerParams(vmem_limit_bytes=VMEM_LIMIT),
    )(every, panel_cover, mine, own_cover)


def local(pixel_ids, quad_offsets, prior_factor):
    row, panel = lax.axis_index("row"), lax.axis_index("panel")
    cell = jnp.stack([pixel_ids % 256, pixel_ids // 256])
    points = (cell[:, None, :] * 8 + quad_offsets).astype(f32)
    quarters = points.reshape(2, Q, 4, 256)[:, :, :, :4].reshape(2, Q, 16)
    lane = jnp.arange(128, dtype=jnp.int32) // 16
    placed = jnp.where(lane == row % 8, jnp.tile(quarters.reshape(32, 16), (1, 8)), 0.0)
    own_rows = lax.dynamic_slice_in_dim(points, panel * 256, 256, 2).transpose(0, 2, 1)
    some_rows = quarters.transpose(0, 2, 1)
    panel_rows = prior_factor.reshape(4, 256, 512)[:, :4].reshape(16, 512)
    every, panel_cover, mine, own_cover = gather(
        panel_rows, prior_factor, placed, own_rows[0], own_rows[1], some_rows[0], some_rows[1]
    )
    return solve(every.reshape(4, B, 512), panel_cover.reshape(4, B, 256), mine, own_cover)


def solution(mesh):
    return jax.shard_map(
        local,
        mesh=mesh,
        in_specs=(P("row"), P(None, None, "row"), P("row", "panel")),
        out_specs=P(("row", "panel"), None),
        check_vma=False,
    )
```

```python
import functools
import math

import jax
import jax.numpy as jnp
from jax import lax
from jax.experimental import pallas as pl
from jax.experimental.pallas import tpu as pltpu
from jax.sharding import PartitionSpec as P

f32, bf16 = jnp.float32, jnp.bfloat16
MESH = pl.DeviceIdType.MESH
NT = (((1,), (1,)), ((), ()))
B = 1024
Q = 16
VMEM_LIMIT = 56 * 2**20
SCALE = -math.log2(math.e) / 64.0


def place():
    row, panel = lax.axis_index("row"), lax.axis_index("panel")
    z = lax.rem(row, 8)
    y = panel // 2 * 2 + lax.rem(row // 8, 2)
    return row // 16, y, z, lax.rem(panel, 2)


def device(x, y, z, core):
    return {"row": (x * 2 + lax.rem(y, 2)) * 8 + z, "panel": y // 2 * 2 + core}


def meet(partners):
    barrier = pltpu.get_barrier_semaphore()
    for partner in partners:
        pl.semaphore_signal(barrier, inc=1, device_id=partner, device_id_type=MESH)
    pl.semaphore_wait(barrier, len(partners))


def send(src, dst, send_sem, recv_sem, target):
    return pltpu.make_async_remote_copy(
        src_ref=src, dst_ref=dst, send_sem=send_sem, recv_sem=recv_sem,
        device_id=target, device_id_type=MESH,
    )


class Ring:
    names = ("sz", "rz", "s2", "r2", "t2", "u2", "s3", "r3", "t3", "u3", "s4", "r4")
    sizes = ((7,), (7,), (2,), (2,), (2,), (2,), (4, 2), (4, 2), (4, 2), (4, 2), (4, 4), (4, 4))

    def __init__(self, own, every, sems):
        self.own, self.every, self.sem = own, every, dict(zip(self.names, sems))
        self.x, self.y, self.z, self.core = place()
        self.row, self.panel = lax.axis_index("row"), lax.axis_index("panel")

    def slab(self, k, i, part=None):
        core, other = self.core, 1 - self.core
        cx = lax.rem(self.x + core * (4 - k) + other * (4 - i), 4)
        cy = lax.rem(self.y + core * (4 - i) + other * (4 - k), 4)
        start = (cx * 2 + lax.rem(cy, 2)) * 8
        blocks = pl.ds(start, 8) if part is None else pl.ds(start + 4 * part, 4)
        return self.every.at[cy // 2 * 2 + core, blocks]

    def neighbour(self, dim, way):
        step = 1 + 2 * way
        along_y = (1 - self.core) if dim == 0 else self.core
        cx = lax.rem(self.x + step * (1 - along_y), 4)
        cy = lax.rem(self.y + step * along_y, 4)
        return device(cx, cy, self.z, self.core)

    def z_copies(self):
        to = [device(self.x, self.y, lax.rem(self.z + d, 8), self.core) for d in range(1, 8)]
        slot = self.every.at[self.panel, self.row]
        return [send(self.own, slot, self.sem["sz"].at[d], self.sem["rz"].at[d], to[d]) for d in range(7)]

    def middle(self):
        part = self.slab(0, 0)
        return [send(part, part, self.sem["s2"].at[w], self.sem["r2"].at[w], self.neighbour(0, w)) for w in range(2)]

    def middle_far(self):
        parts = [self.slab(1, 0, 0), self.slab(3, 0, 1)]
        return [send(parts[w], parts[w], self.sem["t2"].at[w], self.sem["u2"].at[w], self.neighbour(0, w)) for w in range(2)]

    def last(self, k):
        part = self.slab(k, 0)
        return [send(part, part, self.sem["s3"].at[k, w], self.sem["r3"].at[k, w], self.neighbour(1, w)) for w in range(2)]

    def last_far(self, k):
        parts = [self.slab(k, 1, 0), self.slab(k, 3, 1)]
        return [send(parts[w], parts[w], self.sem["t3"].at[k, w], self.sem["u3"].at[k, w], self.neighbour(1, w)) for w in range(2)]

    def hand(self, k, i):
        part = self.slab(k, i)
        twin = device(self.x, self.y, self.z, 1 - self.core)
        return [send(part, part, self.sem["s4"].at[k, i], self.sem["r4"].at[k, i], twin)]

    def all(self):
        copies = self.z_copies() + self.middle() + self.middle_far()
        for k in range(4):
            copies += self.last(k) + self.last_far(k)
        return copies + [c for k in range(4) for i in range(4) for c in self.hand(k, i)]


def begin(*groups):
    for copies in groups:
        for copy in copies:
            copy.start()


def arrive(*groups):
    for copies in groups:
        for copy in copies:
            copy.wait_recv()


def run(step):
    step()


def cover_rows(er, nr, cols, first_tile, tiles, out, i):
    rs = pl.ds(pl.multiple_of(i * 8, 8), 8)
    e8, n8 = er[rs, :], nr[rs, :]
    e = [jnp.broadcast_to(e8[:, a : a + 1], (8, 128)) for a in range(Q)]
    n = [jnp.broadcast_to(n8[:, a : a + 1], (8, 128)) for a in range(Q)]

    def pair(j, _):
        for half in range(2):
            t = 2 * j + half
            acc = [jnp.zeros((8, 128), f32) for _ in range(4)]
            for b in range(Q):
                eb = jnp.broadcast_to(cols[first_tile + t, b : b + 1, :], (8, 128))
                nb = jnp.broadcast_to(cols[first_tile + t, Q + b : Q + b + 1, :], (8, 128))
                for a in range(Q):
                    de, dn = e[a] - eb, n[a] - nb
                    acc[a % 4] = acc[a % 4] + jnp.exp2((de * de + dn * dn) * SCALE)
            cs = pl.ds(pl.multiple_of(t * 128, 128), 128)
            out[rs, cs] = ((acc[0] + acc[1]) + (acc[2] + acc[3])) * (1.0 / (Q * Q))
        return 0

    lax.fori_loop(0, tiles // 2, pair, 0)


def gather_kernel(own, prior, pts, er, nr, se, sn, pe, ce, mine, cover, some, zpts, cols, relay, *sems):
    x, y, z, core = place()
    row, panel = lax.axis_index("row"), lax.axis_index("panel")
    count = len(Ring.names)
    here, psz, prz, ps, pr, qs, qr, qs2, qr2, ts, tr = sems[2 * count :]
    base = row // 8
    y1, ahead, back = y // 2 * 2 + 1 - lax.rem(y, 2), lax.rem(y + 1, 4), lax.rem(y + 3, 4)
    twin = device(x, y, z, 1 - core)
    along = [device(x, y, lax.rem(z + d, 8), core) for d in range(1, 8)]
    meet(
        along
        + [device(lax.rem(x + d, 4), y, z, core) for d in range(1, 4)]
        + [device(lax.rem(x + d, 4), y1, z, core) for d in range(1, 4)]
        + [device(x, ahead, z, core), device(x, back, z, core)]
        + [device(x, ahead, z, 1 - core), device(x, back, z, 1 - core), twin]
    )
    points = [send(pts, zpts.at[d], psz.at[d], prz.at[d], along[d]) for d in range(7)]
    begin(points)
    prior_ring = Ring(own, pe, sems[:count])
    cover_ring = Ring(some, ce, sems[count : 2 * count])
    local_prior = pltpu.make_async_copy(own, pe.at[panel, row], here.at[0])
    local_mine = pltpu.make_async_copy(prior.at[pl.ds(panel * 256, 256)], mine.at[panel], here.at[1])
    local_prior.start()
    local_mine.start()
    begin(prior_ring.z_copies())
    arrive(points)
    total = pts[...]
    for d in range(7):
        total = total + zpts[d]
    cols[base] = total
    spread = [
        send(cols.at[base], cols.at[base], ps.at[d], pr.at[d],
             {"row": lax.rem(base + d + 1, 8) * 8 + z, "panel": panel})
        for d in range(7)
    ]
    begin(spread)
    arrive(spread)
    for i in range(2):
        cover_rows(se, sn, cols, panel * 2, 2, some, i)
    local_cover = pltpu.make_async_copy(some, ce.at[panel, row], here.at[2])
    local_cover.start()
    begin(cover_ring.z_copies())

    def exchange():
        first, second, landing = [], [], []
        for w in range(2):
            to = (ahead, back)[w]
            source = (back, ahead)[w] // 2 * 2 + core
            for c in range(2):
                rows = (1 - y // 2) * 512 + c * 256 + w * 128
                first.append(send(prior.at[pl.ds(rows, 128)], relay.at[w, c], qs.at[w, c], qr.at[w, c],
                                  device(x, to, z, core)))
                hop = functools.partial(send, relay.at[w, c], mine.at[source, pl.ds(w * 128, 128)], qs2.at[w, c])
                second.append(hop(qr2.at[w, core], device(x, to, z, c)))
                landing.append(hop(qr2.at[w, c], device(x, to, z, c)))
        rows = (y // 2 * 2 + 1 - core) * 256
        return first, second, landing, [send(prior.at[pl.ds(rows, 256)], mine.at[panel], ts, tr, twin)]

    def start_ring(ring, local):
        local.wait()
        arrive(ring.z_copies())
        begin(ring.middle(), ring.last(0), ring.hand(0, 0))

    def middle_in(ring):
        arrive(ring.middle())
        begin(ring.middle_far(), ring.last(1), ring.last(3), ring.hand(1, 0), ring.hand(3, 0))

    def middle_far_in(ring):
        arrive(ring.middle_far())
        begin(ring.last(2), ring.hand(2, 0))

    def last_in(ring, *ks):
        for k in ks:
            arrive(ring.last(k))
            begin(ring.last_far(k), ring.hand(k, 1), ring.hand(k, 3))

    def last_far_in(ring):
        for k in range(4):
            arrive(ring.last_far(k))
            begin(ring.hand(k, 2))

    def exchange_out():
        first, _, _, near = exchange()
        begin(first, near)

    def exchange_on():
        first, second, _, _ = exchange()
        arrive(first)
        begin(second)

    steps = {
        0: lambda: start_ring(prior_ring, local_prior),
        2: lambda: start_ring(cover_ring, local_cover),
        4: lambda: middle_in(prior_ring),
        5: lambda: middle_in(cover_ring),
        7: lambda: middle_far_in(prior_ring),
        8: lambda: (middle_far_in(cover_ring), exchange_out()),
        10: lambda: last_in(prior_ring, 0),
        13: lambda: last_in(prior_ring, 1, 3),
        15: lambda: last_in(cover_ring, 0, 1, 3),
        18: lambda: last_in(prior_ring, 2),
        19: lambda: last_in(cover_ring, 2),
        20: exchange_on,
        23: lambda: last_far_in(prior_ring),
        25: lambda: last_far_in(cover_ring),
    }

    def rows(i, _):
        for when, step in steps.items():
            pl.when(i == when)(functools.partial(run, step))
        cover_rows(er, nr, cols, 0, 8, cover, i)
        return 0

    lax.fori_loop(0, 32, rows, 0)
    first, second, landing, near = exchange()
    for ring in (prior_ring, cover_ring):
        for k in range(4):
            for i in range(4):
                arrive(ring.hand(k, i))
    arrive(landing, near)
    local_mine.wait()
    for copy in points + spread + prior_ring.all() + cover_ring.all() + first + second + near:
        copy.wait_send()


def gather(own, prior, pts, er, nr, se, sn):
    dma = pltpu.SemaphoreType.DMA
    hbm, vmem = pl.BlockSpec(memory_space=pl.ANY), pl.BlockSpec(memory_space=pltpu.VMEM)
    ring = [dma(size) for size in Ring.sizes]
    return pl.pallas_call(
        gather_kernel,
        out_shape=[
            jax.ShapeDtypeStruct((4, 64, 16, 512), f32),
            jax.ShapeDtypeStruct((4, 64, 16, 256), f32),
            jax.ShapeDtypeStruct((4, 256, 512), f32),
            jax.ShapeDtypeStruct((256, B), f32),
        ],
        in_specs=[hbm, hbm, vmem, vmem, vmem, vmem, vmem],
        out_specs=[hbm, hbm, hbm, vmem],
        scratch_shapes=[
            pltpu.VMEM((16, 256), f32), pltpu.VMEM((7, 32, 128), f32), pltpu.VMEM((8, 32, 128), f32),
            pltpu.VMEM((2, 2, 128, 512), f32),
            *ring, *ring, dma((3,)), dma((7,)), dma((7,)), dma((7,)), dma((7,)),
            dma((2, 2)), dma((2, 2)), dma((2, 2)), dma((2, 2)), dma, dma,
        ],
        compiler_params=pltpu.CompilerParams(
            collective_id=0, has_side_effects=True, vmem_limit_bytes=VMEM_LIMIT
        ),
    )(own, prior, pts, er, nr, se, sn)


def split(v):
    hi = v.astype(bf16)
    return hi, (v - hi.astype(f32)).astype(bf16)


def dot3(ah, al, bh, bl):
    dot = functools.partial(lax.dot_general, dimension_numbers=NT, preferred_element_type=f32)
    return dot(ah, bh) + (dot(ah, bl) + dot(al, bh))


def factor_inverse(block):
    sub = lax.broadcasted_iota(jnp.int32, (8, 128), 0)
    lane = lax.broadcasted_iota(jnp.int32, (8, 128), 1)
    rest = [block[8 * s : 8 * s + 8, :] for s in range(16)]
    unit = [jnp.where(lane == sub + 8 * s, 1.0, 0.0).astype(f32) for s in range(16)]

    def down(v, k):
        return jnp.broadcast_to(v[k : k + 1, :], (8, 128))

    def across(v, k):
        return jnp.broadcast_to(v[:, k : k + 1], (8, 128))

    out = []
    for s in range(16):
        strip, other = rest[s], unit[s]
        cols = [across(strip, 8 * s + k) for k in range(8)]
        final = jnp.zeros((8, 128), f32)
        for k in range(0, 8, 2):
            upper, lower = sub == k, sub == k + 1
            pair = upper | lower
            p, q, r = down(cols[k], k), down(cols[k + 1], k), down(cols[k + 1], k + 1)
            inverse = 1.0 / (p * r - q * q)
            ip, iq, ir = r * inverse, -(q * inverse), p * inverse
            x, y = cols[k], cols[k + 1]
            cx = jnp.where(upper, -ip, jnp.where(lower, -iq, x * ip + y * iq))
            cy = jnp.where(upper, -iq, jnp.where(lower, -ir, x * iq + y * ir))

            def step(v):
                return jnp.where(pair, 0.0, v) - (cx * down(v, k) + cy * down(v, k + 1))

            root = lax.rsqrt(p)
            ox, oy = down(other, k), down(other, k + 1)
            ratio = q * root * root
            second = (oy - ox * ratio) * lax.rsqrt(r - q * ratio)
            final = jnp.where(upper, ox * root, jnp.where(lower, second, final))
            strip, other = step(strip), step(other)
            for j in range(k + 2, 8):
                cols[j] = step(cols[j])
        out.append(final)
        for t in range(s + 1, 16):
            a, b = rest[t], unit[t]
            for k in range(8):
                c = across(rest[t], 8 * s + k)
                a = a - c * down(strip, k)
                b = b - c * down(other, k)
            rest[t], unit[t] = a, b
    return jnp.concatenate(out, axis=0)


def solve_kernel(every, panel_cover, mine, own_cover, out, raw, ph, lo, m, lh, ll, column, sem):
    row, panel = lax.axis_index("row"), lax.axis_index("panel")
    first = (row * 4 + panel) * 4
    loads = [pltpu.make_async_copy(every.at[p], raw.at[p], sem.at[p]) for p in range(4)]
    for copy in loads:
        copy.start()
    ids = lax.broadcasted_iota(jnp.int32, (256, 256), 0)
    col = lax.broadcasted_iota(jnp.int32, (256, 256), 1)
    unit = jnp.where(ids == col, 1.0, 0.0).astype(f32)
    for j in range(4):
        cj = slice(j * 256, j * 256 + 256)
        own = jnp.where((ids < 4) & (col + j * 256 == first + ids), 1.0, 0.0).astype(f32)
        m[1024:1280, cj] = own_cover[:, cj] + own
        m[cj, cj] = panel_cover[j, cj, :] + unit
        for i in range(j + 1, 4):
            ci = slice(i * 256, i * 256 + 256)
            m[ci, cj] = panel_cover[j, ci, :]
    for p in range(4):
        cp = slice(p * 512, p * 512 + 512)
        ph[1024:1280, cp], lo[1024:1280, cp] = split(mine[p])
    for p in range(4):
        cp = slice(p * 512, p * 512 + 512)
        loads[p].wait()

        def halves(c, _):
            rc = pl.ds(pl.multiple_of(c * 128, 128), 128)
            ph[rc, cp], lo[rc, cp] = split(raw[p, rc, :])
            return 0

        lax.fori_loop(0, 8, halves, 0)

    def update(j, _):
        cj = pl.ds(pl.multiple_of(j * 256, 256), 256)

        def block(i, _):
            ci = pl.ds(pl.multiple_of(i * 256, 256), 256)
            m[ci, cj] = m[ci, cj] - dot3(ph[ci, :], lo[ci, :], ph[cj, :], lo[cj, :])
            return 0

        lax.fori_loop(j, 5, block, 0)
        return 0

    lax.fori_loop(0, 4, update, 0)

    def left(k):
        ck, before = slice(k * 128, k * 128 + 128), slice(0, k * 128)
        for c in range(k // 2, 5):
            rc = slice(c * 256, c * 256 + 256)
            if k == 0:
                column[rc, :] = m[rc, ck]
            else:
                column[rc, :] = m[rc, ck] - dot3(lh[rc, before], ll[rc, before], lh[ck, before], ll[ck, before])

    def right(k, inverse):
        ck = slice(k * 128, k * 128 + 128)
        ih, il = split(inverse)
        for c in range((k + 1) // 2, 5):
            rc = slice(c * 256, c * 256 + 256)
            rh, rl = split(column[rc, :])
            v = dot3(rh, rl, ih, il)
            if c < 4:
                lh[rc, ck], ll[rc, ck] = split(v)
            else:
                if k < 7:
                    lh[rc, ck], ll[rc, ck] = split(v)
                out[:, ck] = v

    left(0)

    def one(k, _):
        inverse = factor_inverse(column[pl.ds(pl.multiple_of(k * 128, 128), 128), :])

        def finish(kk):
            right(kk, inverse)
            if kk < 7:
                left(kk + 1)

        for kk in range(8):
            pl.when(k == kk)(functools.partial(finish, kk))
        return 0

    lax.fori_loop(0, 8, one, 0)


def solve(every, panel_cover, mine, own_cover):
    vmem = pl.BlockSpec(memory_space=pltpu.VMEM)
    return pl.pallas_call(
        solve_kernel,
        out_shape=jax.ShapeDtypeStruct((256, B), f32),
        in_specs=[pl.BlockSpec(memory_space=pl.ANY), vmem, vmem, vmem],
        out_specs=vmem,
        scratch_shapes=[
            pltpu.VMEM((4, B, 512), f32),
            pltpu.VMEM((1280, 2048), bf16), pltpu.VMEM((1280, 2048), bf16),
            pltpu.VMEM((1280, B), f32),
            pltpu.VMEM((1280, B), bf16), pltpu.VMEM((1280, B), bf16),
            pltpu.VMEM((1280, 128), f32), pltpu.SemaphoreType.DMA((4,)),
        ],
        compiler_params=pltpu.CompilerParams(vmem_limit_bytes=VMEM_LIMIT),
    )(every, panel_cover, mine, own_cover)


def local(pixel_ids, quad_offsets, prior_factor):
    row, panel = lax.axis_index("row"), lax.axis_index("panel")
    cell = jnp.stack([pixel_ids % 256, pixel_ids // 256])
    points = (cell[:, None, :] * 8 + quad_offsets).astype(f32)
    quarters = points.reshape(2, Q, 4, 256)[:, :, :, :4].reshape(2, Q, 16)
    lane = jnp.arange(128, dtype=jnp.int32) // 16
    placed = jnp.where(lane == row % 8, jnp.tile(quarters.reshape(32, 16), (1, 8)), 0.0)
    own_rows = lax.dynamic_slice_in_dim(points, panel * 256, 256, 2).transpose(0, 2, 1)
    some_rows = quarters.transpose(0, 2, 1)
    panel_rows = prior_factor.reshape(4, 256, 512)[:, :4].reshape(16, 512)
    every, panel_cover, mine, own_cover = gather(
        panel_rows, prior_factor, placed, own_rows[0], own_rows[1], some_rows[0], some_rows[1]
    )
    return solve(every.reshape(4, B, 512), panel_cover.reshape(4, B, 256), mine, own_cover)


def solution(mesh):
    return jax.shard_map(
        local,
        mesh=mesh,
        in_specs=(P("row"), P(None, None, "row"), P("row", "panel")),
        out_specs=P(("row", "panel"), None),
        check_vma=False,
    )
```

```python
import functools
import math

import jax
import jax.numpy as jnp
from jax import lax
from jax.experimental import pallas as pl
from jax.experimental.pallas import tpu as pltpu
from jax.sharding import PartitionSpec as P

f32, bf16 = jnp.float32, jnp.bfloat16
MESH = pl.DeviceIdType.MESH
NT = (((1,), (1,)), ((), ()))
B = 1024
Q = 16
VMEM_LIMIT = 56 * 2**20
SCALE = -math.log2(math.e) / 64.0


def place():
    row, panel = lax.axis_index("row"), lax.axis_index("panel")
    z = lax.rem(row, 8)
    y = panel // 2 * 2 + lax.rem(row // 8, 2)
    return row // 16, y, z, lax.rem(panel, 2)


def device(x, y, z, core):
    return {"row": (x * 2 + lax.rem(y, 2)) * 8 + z, "panel": y // 2 * 2 + core}


def meet(partners):
    barrier = pltpu.get_barrier_semaphore()
    for partner in partners:
        pl.semaphore_signal(barrier, inc=1, device_id=partner, device_id_type=MESH)
    pl.semaphore_wait(barrier, len(partners))


def send(src, dst, send_sem, recv_sem, target):
    return pltpu.make_async_remote_copy(
        src_ref=src, dst_ref=dst, send_sem=send_sem, recv_sem=recv_sem,
        device_id=target, device_id_type=MESH,
    )


class Ring:
    names = ("sz", "rz", "s2", "r2", "t2", "u2", "s3", "r3", "t3", "u3", "s4", "r4")
    sizes = ((7,), (7,), (2,), (2,), (2,), (2,), (4, 2), (4, 2), (4, 2), (4, 2), (4, 4), (4, 4))

    def __init__(self, own, every, sems, turn):
        self.own, self.every, self.sem = own, every, dict(zip(self.names, sems))
        self.x, self.y, self.z, self.core = place()
        self.turn = turn
        self.row, self.panel = lax.axis_index("row"), lax.axis_index("panel")

    def slab(self, k, i, part=None):
        core, other = self.turn, 1 - self.turn
        cx = lax.rem(self.x + core * (4 - k) + other * (4 - i), 4)
        cy = lax.rem(self.y + core * (4 - i) + other * (4 - k), 4)
        start = (cx * 2 + lax.rem(cy, 2)) * 8
        blocks = pl.ds(start, 8) if part is None else pl.ds(start + 4 * part, 4)
        return self.every.at[cy // 2 * 2 + self.core, blocks]

    def neighbour(self, dim, way):
        step = 1 + 2 * way
        along_y = (1 - self.turn) if dim == 0 else self.turn
        cx = lax.rem(self.x + step * (1 - along_y), 4)
        cy = lax.rem(self.y + step * along_y, 4)
        return device(cx, cy, self.z, self.core)

    def z_copies(self):
        to = [device(self.x, self.y, lax.rem(self.z + d, 8), self.core) for d in range(1, 8)]
        slot = self.every.at[self.panel, self.row]
        return [send(self.own, slot, self.sem["sz"].at[d], self.sem["rz"].at[d], to[d]) for d in range(7)]

    def middle(self):
        part = self.slab(0, 0)
        return [send(part, part, self.sem["s2"].at[w], self.sem["r2"].at[w], self.neighbour(0, w)) for w in range(2)]

    def middle_far(self):
        parts = [self.slab(1, 0, 0), self.slab(3, 0, 1)]
        return [send(parts[w], parts[w], self.sem["t2"].at[w], self.sem["u2"].at[w], self.neighbour(0, w)) for w in range(2)]

    def last(self, k):
        part = self.slab(k, 0)
        return [send(part, part, self.sem["s3"].at[k, w], self.sem["r3"].at[k, w], self.neighbour(1, w)) for w in range(2)]

    def last_far(self, k):
        parts = [self.slab(k, 1, 0), self.slab(k, 3, 1)]
        return [send(parts[w], parts[w], self.sem["t3"].at[k, w], self.sem["u3"].at[k, w], self.neighbour(1, w)) for w in range(2)]

    def hand(self, k, i):
        part = self.slab(k, i)
        twin = device(self.x, self.y, self.z, 1 - self.core)
        return [send(part, part, self.sem["s4"].at[k, i], self.sem["r4"].at[k, i], twin)]

    def all(self):
        copies = self.z_copies() + self.middle() + self.middle_far()
        for k in range(4):
            copies += self.last(k) + self.last_far(k)
        return copies + [c for k in range(4) for i in range(4) for c in self.hand(k, i)]


def begin(*groups):
    for copies in groups:
        for copy in copies:
            copy.start()


def arrive(*groups):
    for copies in groups:
        for copy in copies:
            copy.wait_recv()


def run(step):
    step()


TERMS = 16


def bytes_of(v):
    high = jnp.floor(v * (1.0 / 65536.0)) * 65536.0
    middle = jnp.floor((v - high) * (1.0 / 256.0)) * 256.0
    return high, middle, (v - high) - middle


def row_terms(er, nr, lhs, tiles):
    lane = lax.broadcasted_iota(jnp.int32, (16, 128), 1)

    def tile(i, _):
        rs = pl.ds(pl.multiple_of(i * 8, 8), 8)
        e8, n8 = er[rs, :], nr[rs, :]
        for a in range(0, Q, 2):
            e, n = [
                jnp.concatenate([jnp.broadcast_to(v[:, c : c + 1], (8, 128)) for c in (a, a + 1)]) for v in (e8, n8)
            ]
            eh, nh = jnp.floor(e * 0.125) * 8.0, jnp.floor(n * 0.125) * 8.0
            high, middle, low = bytes_of(e * e + n * n)
            terms = jnp.where(lane < 2, -2.0 * eh, jnp.where(lane < 4, -2.0 * (e - eh), -2.0 * nh))
            terms = jnp.where((lane >= 6) & (lane < 8), -2.0 * (n - nh), terms)
            terms = jnp.where(lane == 8, high, jnp.where(lane == 9, middle, jnp.where(lane == 10, low, terms)))
            terms = jnp.where(lane > 10, jnp.where(lane < 14, 1.0, 0.0), terms)
            lhs[pl.ds(pl.multiple_of(i * 128 + a * 8, 16), 16), :] = terms.astype(bf16)[:, :TERMS]
        return 0

    lax.fori_loop(0, tiles, tile, 0)


def column_terms(cols, rhs, t):
    e, n = cols[t, 0:Q, :], cols[t, Q : 2 * Q, :]
    eh, nh = jnp.floor(e * 0.125) * 8.0, jnp.floor(n * 0.125) * 8.0
    el, nl = e - eh, n - nh
    one, zero = jnp.ones_like(e), jnp.zeros_like(e)
    terms = jnp.stack([eh, el, eh, el, nh, nl, nh, nl, one, one, one, *bytes_of(e * e + n * n), zero, zero])
    rhs[:, :, pl.ds(pl.multiple_of(t * 128, 128), 128)] = jnp.swapaxes(terms, 0, 1).astype(bf16)


def cover_block(lhs, rhs, out, i, tiles, source, target):
    rows = tiles * 128
    left = lhs[pl.ds(pl.multiple_of(i * rows, rows), rows), :]
    acc = [[jnp.zeros((8, 256), f32) for _ in range(2)] for _ in range(tiles)]
    for b in range(Q):
        apart = jnp.dot(left, rhs[b, :, pl.ds(pl.multiple_of(source, 256), 256)], preferred_element_type=f32)
        near = jnp.exp2(apart * SCALE)
        for t in range(tiles):
            for a in range(Q):
                r = t * 128 + a * 8
                acc[t][a % 2] = acc[t][a % 2] + near[r : r + 8, :]
    for t in range(tiles):
        rs = pl.ds(pl.multiple_of(i * tiles * 8 + t * 8, 8), 8)
        out[rs, pl.ds(pl.multiple_of(target, 256), 256)] = (acc[t][0] + acc[t][1]) * (1.0 / (Q * Q))


def gather_kernel(own, prior, pts, er, nr, se, sn, pe, ce, mine, cover, some, zpts, cols, relay, lhs, some_lhs, rhs, *sems):
    x, y, z, core = place()
    row, panel = lax.axis_index("row"), lax.axis_index("panel")
    count = len(Ring.names)
    here, psz, prz, ps, pr, qs, qr, qs2, qr2, ts, tr = sems[2 * count :]
    base = row // 8
    y1, ahead, back = y // 2 * 2 + 1 - lax.rem(y, 2), lax.rem(y + 1, 4), lax.rem(y + 3, 4)
    twin = device(x, y, z, 1 - core)
    along = [device(x, y, lax.rem(z + d, 8), core) for d in range(1, 8)]
    meet(
        along
        + [device(lax.rem(x + d, 4), y, z, core) for d in range(1, 4)]
        + [device(lax.rem(x + d, 4), y1, z, core) for d in range(1, 4)]
        + [device(x, ahead, z, core), device(x, back, z, core)]
        + [device(x, ahead, z, 1 - core), device(x, back, z, 1 - core), twin]
    )
    points = [send(pts, zpts.at[d], psz.at[d], prz.at[d], along[d]) for d in range(7)]
    begin(points)
    prior_ring = Ring(own, pe, sems[:count], 0)
    cover_ring = Ring(some, ce, sems[count : 2 * count], core)
    local_prior = pltpu.make_async_copy(own, pe.at[panel, row], here.at[0])
    local_mine = pltpu.make_async_copy(prior.at[pl.ds(panel * 256, 256)], mine.at[panel], here.at[1])
    local_prior.start()
    local_mine.start()
    begin(prior_ring.z_copies())
    row_terms(se, sn, some_lhs, 2)
    row_terms(er, nr, lhs, 32)
    arrive(points)
    total = pts[...]
    for d in range(7):
        total = total + zpts[d]
    cols[base] = total
    spread = [
        send(cols.at[base], cols.at[base], ps.at[d], pr.at[d],
             {"row": lax.rem(base + d + 1, 8) * 8 + z, "panel": panel})
        for d in range(7)
    ]
    begin(spread)
    arrive(spread)
    for t in range(2):
        column_terms(cols, rhs, panel * 2 + t)
    cover_block(some_lhs, rhs, some, 0, 2, panel * 256, 0)
    local_cover = pltpu.make_async_copy(some, ce.at[panel, row], here.at[2])
    local_cover.start()
    begin(cover_ring.z_copies())

    def others(t, _):
        column_terms(cols, rhs, lax.rem(panel * 2 + t, 8))
        return 0

    lax.fori_loop(2, 8, others, 0)

    def exchange():
        first, second, landing = [], [], []
        for w in range(2):
            to = (ahead, back)[w]
            source = (back, ahead)[w] // 2 * 2 + core
            for c in range(2):
                rows = (1 - y // 2) * 512 + c * 256 + w * 128
                first.append(send(prior.at[pl.ds(rows, 128)], relay.at[w, c], qs.at[w, c], qr.at[w, c],
                                  device(x, to, z, core)))
                hop = functools.partial(send, relay.at[w, c], mine.at[source, pl.ds(w * 128, 128)], qs2.at[w, c])
                second.append(hop(qr2.at[w, core], device(x, to, z, c)))
                landing.append(hop(qr2.at[w, c], device(x, to, z, c)))
        rows = (y // 2 * 2 + 1 - core) * 256
        return first, second, landing, [send(prior.at[pl.ds(rows, 256)], mine.at[panel], ts, tr, twin)]

    def start_ring(ring, local):
        local.wait()
        arrive(ring.z_copies())
        begin(ring.middle(), ring.last(0), ring.hand(0, 0))

    def middle_in(ring):
        arrive(ring.middle())
        begin(ring.middle_far(), ring.last(1), ring.last(3), ring.hand(1, 0), ring.hand(3, 0))

    def middle_far_in(ring):
        arrive(ring.middle_far())
        begin(ring.last(2), ring.hand(2, 0))

    def last_in(ring, *ks):
        for k in ks:
            arrive(ring.last(k))
            begin(ring.last_far(k), ring.hand(k, 1), ring.hand(k, 3))

    def last_far_in(ring):
        for k in range(4):
            arrive(ring.last_far(k))
            begin(ring.hand(k, 2))

    def exchange_out():
        first, _, _, near = exchange()
        begin(first, near)

    def exchange_on():
        first, second, _, _ = exchange()
        arrive(first)
        begin(second)

    steps = {
        0: lambda: start_ring(prior_ring, local_prior),
        3: lambda: start_ring(cover_ring, local_cover),
        6: lambda: middle_in(prior_ring),
        7: lambda: (middle_in(cover_ring), exchange_out()),
        9: lambda: last_in(prior_ring, 0),
        10: lambda: middle_far_in(prior_ring),
        11: lambda: middle_far_in(cover_ring),
        15: lambda: last_in(prior_ring, 1, 3),
        17: lambda: last_in(cover_ring, 0),
        18: exchange_on,
        20: lambda: last_in(prior_ring, 2),
        21: lambda: last_in(cover_ring, 1, 3),
        23: lambda: last_in(cover_ring, 2),
        27: lambda: last_far_in(prior_ring),
        29: lambda: last_far_in(cover_ring),
    }

    def blocks(i, _):
        for when, step in steps.items():
            pl.when(i == when)(functools.partial(run, step))
        at = lax.rem(i, 4) * 256
        cover_block(lhs, rhs, cover, i // 4, 4, at, at)
        return 0

    lax.fori_loop(0, 32, blocks, 0)
    first, second, landing, near = exchange()
    for ring in (prior_ring, cover_ring):
        for k in range(4):
            for i in range(4):
                arrive(ring.hand(k, i))
    arrive(landing, near)
    local_mine.wait()
    for copy in points + spread + prior_ring.all() + cover_ring.all() + first + second + near:
        copy.wait_send()


def gather(own, prior, pts, er, nr, se, sn):
    dma = pltpu.SemaphoreType.DMA
    hbm, vmem = pl.BlockSpec(memory_space=pl.ANY), pl.BlockSpec(memory_space=pltpu.VMEM)
    ring = [dma(size) for size in Ring.sizes]
    return pl.pallas_call(
        gather_kernel,
        out_shape=[
            jax.ShapeDtypeStruct((4, 64, 16, 512), f32),
            jax.ShapeDtypeStruct((4, 64, 16, 256), f32),
            jax.ShapeDtypeStruct((4, 256, 512), f32),
            jax.ShapeDtypeStruct((256, B), f32),
        ],
        in_specs=[hbm, hbm, vmem, vmem, vmem, vmem, vmem],
        out_specs=[hbm, hbm, hbm, vmem],
        scratch_shapes=[
            pltpu.VMEM((16, 256), f32), pltpu.VMEM((7, 32, 128), f32), pltpu.VMEM((8, 32, 128), f32),
            pltpu.VMEM((2, 2, 128, 512), f32),
            pltpu.VMEM((4096, TERMS), bf16), pltpu.VMEM((256, TERMS), bf16), pltpu.VMEM((Q, TERMS, B), bf16),
            *ring, *ring, dma((3,)), dma((7,)), dma((7,)), dma((7,)), dma((7,)),
            dma((2, 2)), dma((2, 2)), dma((2, 2)), dma((2, 2)), dma, dma,
        ],
        compiler_params=pltpu.CompilerParams(
            collective_id=0, has_side_effects=True, vmem_limit_bytes=VMEM_LIMIT
        ),
    )(own, prior, pts, er, nr, se, sn)


def split(v):
    hi = v.astype(bf16)
    return hi, (v - hi.astype(f32)).astype(bf16)


def dot3(ah, al, bh, bl):
    dot = functools.partial(lax.dot_general, dimension_numbers=NT, preferred_element_type=f32)
    return dot(ah, bh) + (dot(ah, bl) + dot(al, bh))


def factor_inverse(block):
    sub = lax.broadcasted_iota(jnp.int32, (8, 128), 0)
    lane = lax.broadcasted_iota(jnp.int32, (8, 128), 1)
    rest = [block[8 * s : 8 * s + 8, :] for s in range(16)]
    unit = [jnp.where(lane == sub + 8 * s, 1.0, 0.0).astype(f32) for s in range(16)]

    def down(v, k):
        return jnp.broadcast_to(v[k : k + 1, :], (8, 128))

    def across(v, k):
        return jnp.broadcast_to(v[:, k : k + 1], (8, 128))

    out = []
    for s in range(16):
        strip, other = rest[s], unit[s]
        cols = [across(strip, 8 * s + k) for k in range(8)]
        final = jnp.zeros((8, 128), f32)
        for k in range(0, 8, 2):
            upper, lower = sub == k, sub == k + 1
            pair = upper | lower
            p, q, r = down(cols[k], k), down(cols[k + 1], k), down(cols[k + 1], k + 1)
            inverse = 1.0 / (p * r - q * q)
            ip, iq, ir = r * inverse, -(q * inverse), p * inverse
            x, y = cols[k], cols[k + 1]
            cx = jnp.where(upper, -ip, jnp.where(lower, -iq, x * ip + y * iq))
            cy = jnp.where(upper, -iq, jnp.where(lower, -ir, x * iq + y * ir))

            def step(v):
                return jnp.where(pair, 0.0, v) - (cx * down(v, k) + cy * down(v, k + 1))

            root = lax.rsqrt(p)
            ox, oy = down(other, k), down(other, k + 1)
            ratio = q * root * root
            second = (oy - ox * ratio) * lax.rsqrt(r - q * ratio)
            final = jnp.where(upper, ox * root, jnp.where(lower, second, final))
            strip, other = step(strip), step(other)
            for j in range(k + 2, 8):
                cols[j] = step(cols[j])
        out.append(final)
        for t in range(s + 1, 16):
            a, b = rest[t], unit[t]
            for k in range(8):
                c = across(rest[t], 8 * s + k)
                a = a - c * down(strip, k)
                b = b - c * down(other, k)
            rest[t], unit[t] = a, b
    return jnp.concatenate(out, axis=0)


def solve_kernel(every, panel_cover, mine, own_cover, out, raw, ph, lo, m, lh, ll, column, sem):
    row, panel = lax.axis_index("row"), lax.axis_index("panel")
    first = (row * 4 + panel) * 4
    loads = [pltpu.make_async_copy(every.at[p], raw.at[p], sem.at[p]) for p in range(4)]
    for copy in loads:
        copy.start()
    ids = lax.broadcasted_iota(jnp.int32, (256, 256), 0)
    col = lax.broadcasted_iota(jnp.int32, (256, 256), 1)
    unit = jnp.where(ids == col, 1.0, 0.0).astype(f32)
    for j in range(4):
        cj = slice(j * 256, j * 256 + 256)
        own = jnp.where((ids < 4) & (col + j * 256 == first + ids), 1.0, 0.0).astype(f32)
        m[1024:1280, cj] = own_cover[:, cj] + own
        m[cj, cj] = panel_cover[j, cj, :] + unit
        for i in range(j + 1, 4):
            ci = slice(i * 256, i * 256 + 256)
            m[ci, cj] = panel_cover[j, ci, :]
    for p in range(4):
        cp = slice(p * 512, p * 512 + 512)
        ph[1024:1280, cp], lo[1024:1280, cp] = split(mine[p])
    for p in range(4):
        cp = slice(p * 512, p * 512 + 512)
        loads[p].wait()

        def halves(c, _):
            rc = pl.ds(pl.multiple_of(c * 128, 128), 128)
            ph[rc, cp], lo[rc, cp] = split(raw[p, rc, :])
            return 0

        lax.fori_loop(0, 8, halves, 0)

    def update(j, _):
        cj = pl.ds(pl.multiple_of(j * 256, 256), 256)

        def block(i, _):
            ci = pl.ds(pl.multiple_of(i * 256, 256), 256)
            m[ci, cj] = m[ci, cj] - dot3(ph[ci, :], lo[ci, :], ph[cj, :], lo[cj, :])
            return 0

        lax.fori_loop(j, 5, block, 0)
        return 0

    lax.fori_loop(0, 4, update, 0)

    def left(k):
        ck, before = slice(k * 128, k * 128 + 128), slice(0, k * 128)
        for c in range(k // 2, 5):
            rc = slice(c * 256, c * 256 + 256)
            if k == 0:
                column[rc, :] = m[rc, ck]
            else:
                column[rc, :] = m[rc, ck] - dot3(lh[rc, before], ll[rc, before], lh[ck, before], ll[ck, before])

    def right(k, inverse):
        ck = slice(k * 128, k * 128 + 128)
        ih, il = split(inverse)
        for c in range((k + 1) // 2, 5):
            rc = slice(c * 256, c * 256 + 256)
            rh, rl = split(column[rc, :])
            v = dot3(rh, rl, ih, il)
            if c < 4:
                lh[rc, ck], ll[rc, ck] = split(v)
            else:
                if k < 7:
                    lh[rc, ck], ll[rc, ck] = split(v)
                out[:, ck] = v

    left(0)

    def one(k, _):
        inverse = factor_inverse(column[pl.ds(pl.multiple_of(k * 128, 128), 128), :])

        def finish(kk):
            right(kk, inverse)
            if kk < 7:
                left(kk + 1)

        for kk in range(8):
            pl.when(k == kk)(functools.partial(finish, kk))
        return 0

    lax.fori_loop(0, 8, one, 0)


def solve(every, panel_cover, mine, own_cover):
    vmem = pl.BlockSpec(memory_space=pltpu.VMEM)
    return pl.pallas_call(
        solve_kernel,
        out_shape=jax.ShapeDtypeStruct((256, B), f32),
        in_specs=[pl.BlockSpec(memory_space=pl.ANY), vmem, vmem, vmem],
        out_specs=vmem,
        scratch_shapes=[
            pltpu.VMEM((4, B, 512), f32),
            pltpu.VMEM((1280, 2048), bf16), pltpu.VMEM((1280, 2048), bf16),
            pltpu.VMEM((1280, B), f32),
            pltpu.VMEM((1280, B), bf16), pltpu.VMEM((1280, B), bf16),
            pltpu.VMEM((1280, 128), f32), pltpu.SemaphoreType.DMA((4,)),
        ],
        compiler_params=pltpu.CompilerParams(vmem_limit_bytes=VMEM_LIMIT),
    )(every, panel_cover, mine, own_cover)


def local(pixel_ids, quad_offsets, prior_factor):
    row, panel = lax.axis_index("row"), lax.axis_index("panel")
    cell = jnp.stack([pixel_ids % 256, pixel_ids // 256])
    points = (cell[:, None, :] * 8 + quad_offsets).astype(f32)
    quarters = points.reshape(2, Q, 4, 256)[:, :, :, :4].reshape(2, Q, 16)
    lane = jnp.arange(128, dtype=jnp.int32) // 16
    placed = jnp.where(lane == row % 8, jnp.tile(quarters.reshape(32, 16), (1, 8)), 0.0)
    own_rows = lax.dynamic_slice_in_dim(points, panel * 256, 256, 2).transpose(0, 2, 1)
    some_rows = quarters.transpose(0, 2, 1)
    panel_rows = prior_factor.reshape(4, 256, 512)[:, :4].reshape(16, 512)
    every, panel_cover, mine, own_cover = gather(
        panel_rows, prior_factor, placed, own_rows[0], own_rows[1], some_rows[0], some_rows[1]
    )
    return solve(every.reshape(4, B, 512), panel_cover.reshape(4, B, 256), mine, own_cover)


def solution(mesh):
    return jax.shard_map(
        local,
        mesh=mesh,
        in_specs=(P("row"), P(None, None, "row"), P("row", "panel")),
        out_specs=P(("row", "panel"), None),
        check_vma=False,
    )
```

```python
import functools
import math

import jax
import jax.numpy as jnp
from jax import lax
from jax.experimental import pallas as pl
from jax.experimental.pallas import tpu as pltpu
from jax.sharding import PartitionSpec as P

f32, bf16 = jnp.float32, jnp.bfloat16
MESH = pl.DeviceIdType.MESH
NT = (((1,), (1,)), ((), ()))
B = 1024
Q = 16
VMEM_LIMIT = 56 * 2**20
SCALE = -math.log2(math.e) / 64.0


def place():
    row, panel = lax.axis_index("row"), lax.axis_index("panel")
    z = lax.rem(row, 8)
    y = panel // 2 * 2 + lax.rem(row // 8, 2)
    return row // 16, y, z, lax.rem(panel, 2)


def device(x, y, z, core):
    return {"row": (x * 2 + lax.rem(y, 2)) * 8 + z, "panel": y // 2 * 2 + core}


def greet(partners):
    barrier = pltpu.get_barrier_semaphore()
    for partner in partners:
        pl.semaphore_signal(barrier, inc=1, device_id=partner, device_id_type=MESH)


def send(src, dst, send_sem, recv_sem, target):
    return pltpu.make_async_remote_copy(
        src_ref=src, dst_ref=dst, send_sem=send_sem, recv_sem=recv_sem,
        device_id=target, device_id_type=MESH,
    )


class Ring:
    names = ("sz", "rz", "s2", "r2", "t2", "u2", "s3", "r3", "t3", "u3", "s4", "r4")
    sizes = ((7,), (7,), (2,), (2,), (2,), (2,), (4, 2), (4, 2), (4, 2), (4, 2), (4, 4), (4, 4))

    def __init__(self, own, every, sems, turn):
        self.own, self.every, self.sem = own, every, dict(zip(self.names, sems))
        self.x, self.y, self.z, self.core = place()
        self.turn = turn
        self.row, self.panel = lax.axis_index("row"), lax.axis_index("panel")

    def slab(self, k, i, part=None):
        core, other = self.turn, 1 - self.turn
        cx = lax.rem(self.x + core * (4 - k) + other * (4 - i), 4)
        cy = lax.rem(self.y + core * (4 - i) + other * (4 - k), 4)
        start = (cx * 2 + lax.rem(cy, 2)) * 8
        blocks = pl.ds(start, 8) if part is None else pl.ds(start + 4 * part, 4)
        return self.every.at[cy // 2 * 2 + self.core, blocks]

    def neighbour(self, dim, way):
        step = 1 + 2 * way
        along_y = (1 - self.turn) if dim == 0 else self.turn
        cx = lax.rem(self.x + step * (1 - along_y), 4)
        cy = lax.rem(self.y + step * along_y, 4)
        return device(cx, cy, self.z, self.core)

    def z_copies(self):
        to = [device(self.x, self.y, lax.rem(self.z + d, 8), self.core) for d in range(1, 8)]
        slot = self.every.at[self.panel, self.row]
        return [send(self.own, slot, self.sem["sz"].at[d], self.sem["rz"].at[d], to[d]) for d in range(7)]

    def middle(self):
        part = self.slab(0, 0)
        return [send(part, part, self.sem["s2"].at[w], self.sem["r2"].at[w], self.neighbour(0, w)) for w in range(2)]

    def middle_far(self):
        parts = [self.slab(1, 0, 0), self.slab(3, 0, 1)]
        return [send(parts[w], parts[w], self.sem["t2"].at[w], self.sem["u2"].at[w], self.neighbour(0, w)) for w in range(2)]

    def last(self, k):
        part = self.slab(k, 0)
        return [send(part, part, self.sem["s3"].at[k, w], self.sem["r3"].at[k, w], self.neighbour(1, w)) for w in range(2)]

    def last_far(self, k):
        parts = [self.slab(k, 1, 0), self.slab(k, 3, 1)]
        return [send(parts[w], parts[w], self.sem["t3"].at[k, w], self.sem["u3"].at[k, w], self.neighbour(1, w)) for w in range(2)]

    def hand(self, k, i):
        part = self.slab(k, i)
        twin = device(self.x, self.y, self.z, 1 - self.core)
        return [send(part, part, self.sem["s4"].at[k, i], self.sem["r4"].at[k, i], twin)]

    def all(self):
        copies = self.z_copies() + self.middle() + self.middle_far()
        for k in range(4):
            copies += self.last(k) + self.last_far(k)
        return copies + [c for k in range(4) for i in range(4) for c in self.hand(k, i)]


def begin(*groups):
    for copies in groups:
        for copy in copies:
            copy.start()


def arrive(*groups):
    for copies in groups:
        for copy in copies:
            copy.wait_recv()


def run(step):
    step()


TERMS = 16


def bytes_of(v):
    high = jnp.floor(v * (1.0 / 65536.0)) * 65536.0
    middle = jnp.floor((v - high) * (1.0 / 256.0)) * 256.0
    return high, middle, (v - high) - middle


def row_terms(rows, lhs, tiles):
    lane = lax.broadcasted_iota(jnp.int32, (16, 128), 1)

    def tile(i, _):
        rs = pl.ds(pl.multiple_of(i * 8, 8), 8)
        both = rows[rs, :]
        for a in range(0, Q, 2):
            e, n = [
                jnp.concatenate([jnp.broadcast_to(both[:, c : c + 1], (8, 128)) for c in (o + a, o + a + 1)])
                for o in (0, Q)
            ]
            eh, nh = jnp.floor(e * 0.125) * 8.0, jnp.floor(n * 0.125) * 8.0
            high, middle, low = bytes_of(e * e + n * n)
            terms = jnp.where(lane < 2, -2.0 * eh, jnp.where(lane < 4, -2.0 * (e - eh), -2.0 * nh))
            terms = jnp.where((lane >= 6) & (lane < 8), -2.0 * (n - nh), terms)
            terms = jnp.where(lane == 8, high, jnp.where(lane == 9, middle, jnp.where(lane == 10, low, terms)))
            terms = jnp.where(lane > 10, jnp.where(lane < 14, 1.0, 0.0), terms)
            lhs[pl.ds(pl.multiple_of(i * 128 + a * 8, 16), 16), :] = terms.astype(bf16)[:, :TERMS]
        return 0

    lax.fori_loop(0, tiles, tile, 0)


def points_of(ids, offsets, lanes):
    cell = ids[:, lanes]
    east = (cell & 255) * 8 + offsets[0, :, lanes]
    north = (cell >> 8) * 8 + offsets[1, :, lanes]
    return jnp.concatenate([east, north]).astype(f32)


def prepare(ids, offsets, pts, rows, some_rows, z, panel):
    lane = lax.broadcasted_iota(jnp.int32, (2 * Q, 128), 1)
    few = jnp.zeros((2 * Q, 128), f32)
    for q in range(4):
        quarter = points_of(ids, offsets, slice(q * 256, q * 256 + 128))
        moved = quarter if q == 0 else pltpu.roll(quarter, 4 * q, 1)
        few = jnp.where((lane >= 4 * q) & (lane < 4 * q + 4), moved, few)
    again = few
    for shift in (16, 32, 64):
        again = again + pltpu.roll(again, shift, 1)
    pts[...] = jnp.where(lane // 16 == z, again, 0.0)
    blank = jnp.zeros((128 - 2 * Q, 128), f32)
    some_rows[...] = jnp.transpose(jnp.concatenate([few, blank]))[0:16, :]
    for h in range(2):
        own = points_of(ids, offsets, pl.ds(pl.multiple_of(panel * 256 + h * 128, 128), 128))
        rows[h * 128 : h * 128 + 128, :] = jnp.transpose(jnp.concatenate([own, blank]))


def column_terms(cols, rhs, t):
    e, n = cols[t, 0:Q, :], cols[t, Q : 2 * Q, :]
    eh, nh = jnp.floor(e * 0.125) * 8.0, jnp.floor(n * 0.125) * 8.0
    el, nl = e - eh, n - nh
    one, zero = jnp.ones_like(e), jnp.zeros_like(e)
    terms = jnp.stack([eh, el, eh, el, nh, nl, nh, nl, one, one, one, *bytes_of(e * e + n * n), zero, zero])
    rhs[:, :, pl.ds(pl.multiple_of(t * 128, 128), 128)] = jnp.swapaxes(terms, 0, 1).astype(bf16)


def cover_block(lhs, rhs, out, i, tiles, source, target):
    rows = tiles * 128
    left = lhs[pl.ds(pl.multiple_of(i * rows, rows), rows), :]
    acc = [[jnp.zeros((8, 256), f32) for _ in range(2)] for _ in range(tiles)]
    for b in range(Q):
        apart = jnp.dot(left, rhs[b, :, pl.ds(pl.multiple_of(source, 256), 256)], preferred_element_type=f32)
        near = jnp.exp2(apart * SCALE)
        for t in range(tiles):
            for a in range(Q):
                r = t * 128 + a * 8
                acc[t][a % 2] = acc[t][a % 2] + near[r : r + 8, :]
    for t in range(tiles):
        rs = pl.ds(pl.multiple_of(i * tiles * 8 + t * 8, 8), 8)
        out[rs, pl.ds(pl.multiple_of(target, 256), 256)] = (acc[t][0] + acc[t][1]) * (1.0 / (Q * Q))


def gather_kernel(ids, offsets, prior, pe, ce, mine, cover, pts, rows, some_rows, ends, own, some, zpts, cols, relay,
                  lhs, some_lhs, rhs, *sems):
    x, y, z, core = place()
    row, panel = lax.axis_index("row"), lax.axis_index("panel")
    count = len(Ring.names)
    quarters, here, psz, prz, ps, pr, qs, qr, qs2, qr2, ts, tr = sems[2 * count :]
    base = row // 8
    y1, ahead, back = y // 2 * 2 + 1 - lax.rem(y, 2), lax.rem(y + 1, 4), lax.rem(y + 3, 4)
    twin = device(x, y, z, 1 - core)
    along = [device(x, y, lax.rem(z + d, 8), core) for d in range(1, 8)]
    greeted = (
        along
        + [device(lax.rem(x + d, 4), y, z, core) for d in range(1, 4)]
        + [device(lax.rem(x + d, 4), y1, z, core) for d in range(1, 4)]
        + [device(x, ahead, z, core), device(x, back, z, core)]
        + [device(x, ahead, z, 1 - core), device(x, back, z, 1 - core), twin]
    )
    tops = [pltpu.make_async_copy(prior.at[pl.ds(q * 256, 8)], ends.at[q], quarters.at[q]) for q in range(4)]
    for copy in tops:
        copy.start()
    greet(greeted)
    prepare(ids, offsets, pts, rows, some_rows, z, panel)
    for copy in tops:
        copy.wait()
    for h in range(2):
        own[h * 8 : h * 8 + 8, :] = jnp.concatenate([ends[2 * h, 0:4, :], ends[2 * h + 1, 0:4, :]])
    pl.semaphore_wait(pltpu.get_barrier_semaphore(), len(greeted))
    points = [send(pts, zpts.at[d], psz.at[d], prz.at[d], along[d]) for d in range(7)]
    begin(points)
    prior_ring = Ring(own, pe, sems[:count], 0)
    cover_ring = Ring(some, ce, sems[count : 2 * count], core)
    local_prior = pltpu.make_async_copy(own, pe.at[panel, row], here.at[0])
    local_mine = pltpu.make_async_copy(prior.at[pl.ds(panel * 256, 256)], mine.at[panel], here.at[1])
    local_prior.start()
    local_mine.start()
    begin(prior_ring.z_copies())
    row_terms(some_rows, some_lhs, 2)
    arrive(points)
    total = pts[...]
    for d in range(7):
        total = total + zpts[d]
    cols[base] = total
    spread = [
        send(cols.at[base], cols.at[base], ps.at[d], pr.at[d],
             {"row": lax.rem(base + d + 1, 8) * 8 + z, "panel": panel})
        for d in range(7)
    ]
    begin(spread)

    def start_ring(ring, local):
        local.wait()
        arrive(ring.z_copies())
        begin(ring.middle(), ring.last(0), ring.hand(0, 0))

    start_ring(prior_ring, local_prior)
    row_terms(rows, lhs, 32)
    arrive(spread)
    for t in range(2):
        column_terms(cols, rhs, panel * 2 + t)
    cover_block(some_lhs, rhs, some, 0, 2, panel * 256, 0)
    local_cover = pltpu.make_async_copy(some, ce.at[panel, row], here.at[2])
    local_cover.start()
    begin(cover_ring.z_copies())

    def others(t, _):
        column_terms(cols, rhs, lax.rem(panel * 2 + t, 8))
        return 0

    lax.fori_loop(2, 8, others, 0)

    def exchange():
        first, second, landing = [], [], []
        for w in range(2):
            to = (ahead, back)[w]
            source = (back, ahead)[w] // 2 * 2 + core
            for c in range(2):
                rows = (1 - y // 2) * 512 + c * 256 + w * 128
                first.append(send(prior.at[pl.ds(rows, 128)], relay.at[w, c], qs.at[w, c], qr.at[w, c],
                                  device(x, to, z, core)))
                hop = functools.partial(send, relay.at[w, c], mine.at[source, pl.ds(w * 128, 128)], qs2.at[w, c])
                second.append(hop(qr2.at[w, core], device(x, to, z, c)))
                landing.append(hop(qr2.at[w, c], device(x, to, z, c)))
        rows = (y // 2 * 2 + 1 - core) * 256
        return first, second, landing, [send(prior.at[pl.ds(rows, 256)], mine.at[panel], ts, tr, twin)]

    def middle_in(ring):
        arrive(ring.middle())
        begin(ring.middle_far(), ring.last(1), ring.last(3), ring.hand(1, 0), ring.hand(3, 0))

    def middle_far_in(ring):
        arrive(ring.middle_far())
        begin(ring.last(2), ring.hand(2, 0))

    def last_in(ring, *ks):
        for k in ks:
            arrive(ring.last(k))
            begin(ring.last_far(k), ring.hand(k, 1), ring.hand(k, 3))

    def last_far_in(ring):
        for k in range(4):
            arrive(ring.last_far(k))
            begin(ring.hand(k, 2))

    def exchange_out():
        first, _, _, near = exchange()
        begin(first, near)

    def exchange_on():
        first, second, _, _ = exchange()
        arrive(first)
        begin(second)

    steps = {
        0: lambda: middle_in(prior_ring),
        1: lambda: start_ring(cover_ring, local_cover),
        2: lambda: last_in(prior_ring, 0),
        4: lambda: middle_far_in(prior_ring),
        5: lambda: (middle_in(cover_ring), exchange_out()),
        8: lambda: middle_far_in(cover_ring),
        9: lambda: last_in(prior_ring, 1, 3),
        13: lambda: last_in(cover_ring, 0),
        14: lambda: last_in(prior_ring, 2),
        15: exchange_on,
        17: lambda: last_in(cover_ring, 1, 3),
        20: lambda: last_in(cover_ring, 2),
        22: lambda: last_far_in(prior_ring),
        27: lambda: last_far_in(cover_ring),
    }

    def blocks(i, _):
        for when, step in steps.items():
            pl.when(i == when)(functools.partial(run, step))
        at = lax.rem(i, 4) * 256
        cover_block(lhs, rhs, cover, i // 4, 4, at, at)
        return 0

    lax.fori_loop(0, 32, blocks, 0)
    first, second, landing, near = exchange()
    for ring in (prior_ring, cover_ring):
        for k in range(4):
            for i in range(4):
                arrive(ring.hand(k, i))
    arrive(landing, near)
    local_mine.wait()
    for copy in points + spread + prior_ring.all() + cover_ring.all() + first + second + near:
        copy.wait_send()


def gather(ids, offsets, prior):
    dma = pltpu.SemaphoreType.DMA
    hbm, vmem = pl.BlockSpec(memory_space=pl.ANY), pl.BlockSpec(memory_space=pltpu.VMEM)
    ring = [dma(size) for size in Ring.sizes]
    return pl.pallas_call(
        gather_kernel,
        out_shape=[
            jax.ShapeDtypeStruct((4, 64, 16, 512), f32),
            jax.ShapeDtypeStruct((4, 64, 16, 256), f32),
            jax.ShapeDtypeStruct((4, 256, 512), f32),
            jax.ShapeDtypeStruct((256, B), f32),
        ],
        in_specs=[vmem, vmem, hbm],
        out_specs=[hbm, hbm, hbm, vmem],
        scratch_shapes=[
            pltpu.VMEM((32, 128), f32), pltpu.VMEM((256, 128), f32), pltpu.VMEM((16, 128), f32),
            pltpu.VMEM((4, 8, 512), f32), pltpu.VMEM((16, 512), f32),
            pltpu.VMEM((16, 256), f32), pltpu.VMEM((7, 32, 128), f32), pltpu.VMEM((8, 32, 128), f32),
            pltpu.VMEM((2, 2, 128, 512), f32),
            pltpu.VMEM((4096, TERMS), bf16), pltpu.VMEM((256, TERMS), bf16), pltpu.VMEM((Q, TERMS, B), bf16),
            *ring, *ring, dma((4,)), dma((3,)), dma((7,)), dma((7,)), dma((7,)), dma((7,)),
            dma((2, 2)), dma((2, 2)), dma((2, 2)), dma((2, 2)), dma, dma,
        ],
        compiler_params=pltpu.CompilerParams(
            collective_id=0, has_side_effects=True, vmem_limit_bytes=VMEM_LIMIT
        ),
    )(ids, offsets, prior)


def split(v):
    hi = v.astype(bf16)
    return hi, (v - hi.astype(f32)).astype(bf16)


def dot3(ah, al, bh, bl):
    dot = functools.partial(lax.dot_general, dimension_numbers=NT, preferred_element_type=f32)
    return dot(ah, bh) + (dot(ah, bl) + dot(al, bh))


def factor_inverse(block):
    sub = lax.broadcasted_iota(jnp.int32, (8, 128), 0)
    lane = lax.broadcasted_iota(jnp.int32, (8, 128), 1)
    rest = [block[8 * s : 8 * s + 8, :] for s in range(16)]
    unit = [jnp.where(lane == sub + 8 * s, 1.0, 0.0).astype(f32) for s in range(16)]

    def down(v, k):
        return jnp.broadcast_to(v[k : k + 1, :], (8, 128))

    def across(v, k):
        return jnp.broadcast_to(v[:, k : k + 1], (8, 128))

    out = []
    for s in range(16):
        strip, other = rest[s], unit[s]
        cols = [across(strip, 8 * s + k) for k in range(8)]
        final = jnp.zeros((8, 128), f32)
        for k in range(0, 8, 2):
            upper, lower = sub == k, sub == k + 1
            pair = upper | lower
            p, q, r = down(cols[k], k), down(cols[k + 1], k), down(cols[k + 1], k + 1)
            inverse = 1.0 / (p * r - q * q)
            ip, iq, ir = r * inverse, -(q * inverse), p * inverse
            x, y = cols[k], cols[k + 1]
            cx = jnp.where(upper, -ip, jnp.where(lower, -iq, x * ip + y * iq))
            cy = jnp.where(upper, -iq, jnp.where(lower, -ir, x * iq + y * ir))

            def step(v):
                return jnp.where(pair, 0.0, v) - (cx * down(v, k) + cy * down(v, k + 1))

            root = lax.rsqrt(p)
            ox, oy = down(other, k), down(other, k + 1)
            ratio = q * root * root
            second = (oy - ox * ratio) * lax.rsqrt(r - q * ratio)
            final = jnp.where(upper, ox * root, jnp.where(lower, second, final))
            strip, other = step(strip), step(other)
            for j in range(k + 2, 8):
                cols[j] = step(cols[j])
        out.append(final)
        for t in range(s + 1, 16):
            a, b = rest[t], unit[t]
            for k in range(8):
                c = across(rest[t], 8 * s + k)
                a = a - c * down(strip, k)
                b = b - c * down(other, k)
            rest[t], unit[t] = a, b
    return jnp.concatenate(out, axis=0)


def solve_kernel(every, panel_cover, mine, own_cover, out, raw, raw_mine, ph, lo, m, lh, ll, column, sem):
    row, panel = lax.axis_index("row"), lax.axis_index("panel")
    first = (row * 4 + panel) * 4
    loads = [pltpu.make_async_copy(every.at[p], raw.at[p], sem.at[p]) for p in range(4)]
    load_mine = pltpu.make_async_copy(mine, raw_mine, sem.at[4])
    load_own = pltpu.make_async_copy(own_cover, m.at[pl.ds(1024, 256)], sem.at[5])
    load_cover = [
        pltpu.make_async_copy(
            panel_cover.at[j, pl.ds(j * 256, B - j * 256)],
            m.at[pl.ds(j * 256, B - j * 256), pl.ds(j * 256, 256)],
            sem.at[6 + j],
        )
        for j in range(4)
    ]
    for copy in [*loads, load_mine, load_own, *load_cover]:
        copy.start()
    for p in range(4):
        cp = slice(p * 512, p * 512 + 512)
        loads[p].wait()

        def halves(c, _):
            rc = pl.ds(pl.multiple_of(c * 128, 128), 128)
            ph[rc, cp], lo[rc, cp] = split(raw[p, rc, :])
            return 0

        lax.fori_loop(0, 8, halves, 0)

    load_mine.wait()
    for p in range(4):
        cp = slice(p * 512, p * 512 + 512)
        ph[1024:1280, cp], lo[1024:1280, cp] = split(raw_mine[p])
    load_own.wait()
    for copy in load_cover:
        copy.wait()
    ids = lax.broadcasted_iota(jnp.int32, (256, 256), 0)
    col = lax.broadcasted_iota(jnp.int32, (256, 256), 1)
    unit = jnp.where(ids == col, 1.0, 0.0).astype(f32)
    for j in range(4):
        cj = slice(j * 256, j * 256 + 256)
        own = jnp.where((ids < 4) & (col + j * 256 == first + ids), 1.0, 0.0).astype(f32)
        m[1024:1280, cj] = m[1024:1280, cj] + own
        m[cj, cj] = m[cj, cj] + unit

    def update(j, _):
        cj = pl.ds(pl.multiple_of(j * 256, 256), 256)

        def block(i, _):
            ci = pl.ds(pl.multiple_of(i * 256, 256), 256)
            m[ci, cj] = m[ci, cj] - dot3(ph[ci, :], lo[ci, :], ph[cj, :], lo[cj, :])
            return 0

        lax.fori_loop(j, 5, block, 0)
        return 0

    lax.fori_loop(0, 4, update, 0)

    def left(k):
        ck, before = slice(k * 128, k * 128 + 128), slice(0, k * 128)
        for c in range(k // 2, 5):
            rc = slice(c * 256, c * 256 + 256)
            if k == 0:
                column[rc, :] = m[rc, ck]
            else:
                column[rc, :] = m[rc, ck] - dot3(lh[rc, before], ll[rc, before], lh[ck, before], ll[ck, before])

    def right(k, inverse):
        ck = slice(k * 128, k * 128 + 128)
        ih, il = split(inverse)
        for c in range((k + 1) // 2, 5):
            rc = slice(c * 256, c * 256 + 256)
            rh, rl = split(column[rc, :])
            v = dot3(rh, rl, ih, il)
            if c < 4:
                lh[rc, ck], ll[rc, ck] = split(v)
            else:
                if k < 7:
                    lh[rc, ck], ll[rc, ck] = split(v)
                out[:, ck] = v

    left(0)

    def one(k, _):
        inverse = factor_inverse(column[pl.ds(pl.multiple_of(k * 128, 128), 128), :])

        def finish(kk):
            right(kk, inverse)
            if kk < 7:
                left(kk + 1)

        for kk in range(8):
            pl.when(k == kk)(functools.partial(finish, kk))
        return 0

    lax.fori_loop(0, 8, one, 0)


def solve(every, panel_cover, mine, own_cover):
    vmem = pl.BlockSpec(memory_space=pltpu.VMEM)
    return pl.pallas_call(
        solve_kernel,
        out_shape=jax.ShapeDtypeStruct((256, B), f32),
        in_specs=[pl.BlockSpec(memory_space=pl.ANY)] * 4,
        out_specs=vmem,
        scratch_shapes=[
            pltpu.VMEM((4, B, 512), f32), pltpu.VMEM((4, 256, 512), f32),
            pltpu.VMEM((1280, 2048), bf16), pltpu.VMEM((1280, 2048), bf16),
            pltpu.VMEM((1280, B), f32),
            pltpu.VMEM((1280, B), bf16), pltpu.VMEM((1280, B), bf16),
            pltpu.VMEM((1280, 128), f32), pltpu.SemaphoreType.DMA((10,)),
        ],
        compiler_params=pltpu.CompilerParams(vmem_limit_bytes=VMEM_LIMIT),
    )(every, panel_cover, mine, own_cover)


def local(pixel_ids, quad_offsets, prior_factor):
    every, panel_cover, mine, own_cover = gather(pixel_ids.reshape(1, 1024), quad_offsets, prior_factor)
    return solve(every.reshape(4, B, 512), panel_cover.reshape(4, B, 256), mine, own_cover)


def solution(mesh):
    return jax.shard_map(
        local,
        mesh=mesh,
        in_specs=(P("row"), P(None, None, "row"), P("row", "panel")),
        out_specs=P(("row", "panel"), None),
        check_vma=False,
    )
```

```python
import functools
import math

import jax
import jax.numpy as jnp
from jax import lax
from jax.experimental import pallas as pl
from jax.experimental.pallas import tpu as pltpu
from jax.sharding import PartitionSpec as P

f32, bf16 = jnp.float32, jnp.bfloat16
MESH = pl.DeviceIdType.MESH
NT = (((1,), (1,)), ((), ()))
B = 1024
Q = 16
VMEM_LIMIT = 56 * 2**20
SCALE = -math.log2(math.e) / 64.0


def place():
    row, panel = lax.axis_index("row"), lax.axis_index("panel")
    z = lax.rem(row, 8)
    y = panel // 2 * 2 + lax.rem(row // 8, 2)
    return row // 16, y, z, lax.rem(panel, 2)


def device(x, y, z, core):
    return {"row": (x * 2 + lax.rem(y, 2)) * 8 + z, "panel": y // 2 * 2 + core}


def greet(partners):
    barrier = pltpu.get_barrier_semaphore()
    for partner in partners:
        pl.semaphore_signal(barrier, inc=1, device_id=partner, device_id_type=MESH)


def send(src, dst, send_sem, recv_sem, target):
    return pltpu.make_async_remote_copy(
        src_ref=src, dst_ref=dst, send_sem=send_sem, recv_sem=recv_sem,
        device_id=target, device_id_type=MESH,
    )


class Ring:
    names = ("sz", "rz", "s2", "r2", "t2", "u2", "s3", "r3", "t3", "u3", "s4", "r4")
    sizes = ((7,), (7,), (2,), (2,), (2,), (2,), (4, 2), (4, 2), (4, 2), (4, 2), (4, 4), (4, 4))

    def __init__(self, own, every, sems, turn):
        self.own, self.every, self.sem = own, every, dict(zip(self.names, sems))
        self.x, self.y, self.z, self.core = place()
        self.turn = turn
        self.row, self.panel = lax.axis_index("row"), lax.axis_index("panel")

    def slab(self, k, i, part=None):
        core, other = self.turn, 1 - self.turn
        cx = lax.rem(self.x + core * (4 - k) + other * (4 - i), 4)
        cy = lax.rem(self.y + core * (4 - i) + other * (4 - k), 4)
        start = (cx * 2 + lax.rem(cy, 2)) * 8
        blocks = pl.ds(start, 8) if part is None else pl.ds(start + 4 * part, 4)
        return self.every.at[cy // 2 * 2 + self.core, blocks]

    def neighbour(self, dim, way):
        step = 1 + 2 * way
        along_y = (1 - self.turn) if dim == 0 else self.turn
        cx = lax.rem(self.x + step * (1 - along_y), 4)
        cy = lax.rem(self.y + step * along_y, 4)
        return device(cx, cy, self.z, self.core)

    def z_copies(self):
        to = [device(self.x, self.y, lax.rem(self.z + d, 8), self.core) for d in range(1, 8)]
        slot = self.every.at[self.panel, self.row]
        return [send(self.own, slot, self.sem["sz"].at[d], self.sem["rz"].at[d], to[d]) for d in range(7)]

    def middle(self):
        part = self.slab(0, 0)
        return [send(part, part, self.sem["s2"].at[w], self.sem["r2"].at[w], self.neighbour(0, w)) for w in range(2)]

    def middle_far(self):
        parts = [self.slab(1, 0, 0), self.slab(3, 0, 1)]
        return [send(parts[w], parts[w], self.sem["t2"].at[w], self.sem["u2"].at[w], self.neighbour(0, w)) for w in range(2)]

    def last(self, k):
        part = self.slab(k, 0)
        return [send(part, part, self.sem["s3"].at[k, w], self.sem["r3"].at[k, w], self.neighbour(1, w)) for w in range(2)]

    def last_far(self, k):
        parts = [self.slab(k, 1, 0), self.slab(k, 3, 1)]
        return [send(parts[w], parts[w], self.sem["t3"].at[k, w], self.sem["u3"].at[k, w], self.neighbour(1, w)) for w in range(2)]

    def hand(self, k, i):
        part = self.slab(k, i)
        twin = device(self.x, self.y, self.z, 1 - self.core)
        return [send(part, part, self.sem["s4"].at[k, i], self.sem["r4"].at[k, i], twin)]

    def all(self):
        copies = self.z_copies() + self.middle() + self.middle_far()
        for k in range(4):
            copies += self.last(k) + self.last_far(k)
        return copies + [c for k in range(4) for i in range(4) for c in self.hand(k, i)]


def begin(*groups):
    for copies in groups:
        for copy in copies:
            copy.start()


def arrive(*groups):
    for copies in groups:
        for copy in copies:
            copy.wait_recv()


def run(step):
    step()


TERMS = 16


def bytes_of(v):
    high = jnp.floor(v * (1.0 / 65536.0)) * 65536.0
    middle = jnp.floor((v - high) * (1.0 / 256.0)) * 256.0
    return high, middle, (v - high) - middle


def row_terms(rows, lhs, tiles):
    lane = lax.broadcasted_iota(jnp.int32, (16, 128), 1)

    def tile(i, _):
        rs = pl.ds(pl.multiple_of(i * 8, 8), 8)
        both = rows[rs, :]
        for a in range(0, Q, 2):
            e, n = [
                jnp.concatenate([jnp.broadcast_to(both[:, c : c + 1], (8, 128)) for c in (o + a, o + a + 1)])
                for o in (0, Q)
            ]
            eh, nh = jnp.floor(e * 0.125) * 8.0, jnp.floor(n * 0.125) * 8.0
            high, middle, low = bytes_of(e * e + n * n)
            terms = jnp.where(lane < 2, -2.0 * eh, jnp.where(lane < 4, -2.0 * (e - eh), -2.0 * nh))
            terms = jnp.where((lane >= 6) & (lane < 8), -2.0 * (n - nh), terms)
            terms = jnp.where(lane == 8, high, jnp.where(lane == 9, middle, jnp.where(lane == 10, low, terms)))
            terms = jnp.where(lane > 10, jnp.where(lane < 14, 1.0, 0.0), terms)
            lhs[pl.ds(pl.multiple_of(i * 128 + a * 8, 16), 16), :] = terms.astype(bf16)[:, :TERMS]
        return 0

    lax.fori_loop(0, tiles, tile, 0)


def points_of(ids, offsets, lanes):
    cell = ids[:, lanes]
    east = (cell & 255) * 8 + offsets[0, :, lanes]
    north = (cell >> 8) * 8 + offsets[1, :, lanes]
    return jnp.concatenate([east, north]).astype(f32)


def prepare(ids, offsets, pts, rows, some_rows, z, panel):
    lane = lax.broadcasted_iota(jnp.int32, (2 * Q, 128), 1)
    few = jnp.zeros((2 * Q, 128), f32)
    for q in range(4):
        quarter = points_of(ids, offsets, slice(q * 256, q * 256 + 128))
        moved = quarter if q == 0 else pltpu.roll(quarter, 4 * q, 1)
        few = jnp.where((lane >= 4 * q) & (lane < 4 * q + 4), moved, few)
    again = few
    for shift in (16, 32, 64):
        again = again + pltpu.roll(again, shift, 1)
    pts[...] = jnp.where(lane // 16 == z, again, 0.0)
    blank = jnp.zeros((128 - 2 * Q, 128), f32)
    some_rows[...] = jnp.transpose(jnp.concatenate([few, blank]))[0:16, :]
    for h in range(2):
        own = points_of(ids, offsets, pl.ds(pl.multiple_of(panel * 256 + h * 128, 128), 128))
        rows[h * 128 : h * 128 + 128, :] = jnp.transpose(jnp.concatenate([own, blank]))


def column_terms(cols, rhs, t):
    e, n = cols[t, 0:Q, :], cols[t, Q : 2 * Q, :]
    eh, nh = jnp.floor(e * 0.125) * 8.0, jnp.floor(n * 0.125) * 8.0
    el, nl = e - eh, n - nh
    one, zero = jnp.ones_like(e), jnp.zeros_like(e)
    terms = jnp.stack([eh, el, eh, el, nh, nl, nh, nl, one, one, one, *bytes_of(e * e + n * n), zero, zero])
    rhs[:, :, pl.ds(pl.multiple_of(t * 128, 128), 128)] = jnp.swapaxes(terms, 0, 1).astype(bf16)


def cover_block(lhs, rhs, out, i, tiles, source, target):
    rows = tiles * 128
    left = lhs[pl.ds(pl.multiple_of(i * rows, rows), rows), :]
    acc = [[jnp.zeros((8, 256), f32) for _ in range(2)] for _ in range(tiles)]
    for b in range(Q):
        apart = jnp.dot(left, rhs[b, :, pl.ds(pl.multiple_of(source, 256), 256)], preferred_element_type=f32)
        near = jnp.exp2(apart * SCALE)
        for t in range(tiles):
            for a in range(Q):
                r = t * 128 + a * 8
                acc[t][a % 2] = acc[t][a % 2] + near[r : r + 8, :]
    for t in range(tiles):
        rs = pl.ds(pl.multiple_of(i * tiles * 8 + t * 8, 8), 8)
        out[rs, pl.ds(pl.multiple_of(target, 256), 256)] = (acc[t][0] + acc[t][1]) * (1.0 / (Q * Q))


def gather_kernel(ids, offsets, prior, pe, ce, mine, cover, pts, rows, some_rows, ends, own, some, zpts, cols, relay,
                  lhs, some_lhs, rhs, *sems):
    x, y, z, core = place()
    row, panel = lax.axis_index("row"), lax.axis_index("panel")
    count = len(Ring.names)
    quarters, here, psz, prz, ps, pr, qs, qr, qs2, qr2, ts, tr = sems[2 * count :]
    base = row // 8
    y1, ahead, back = y // 2 * 2 + 1 - lax.rem(y, 2), lax.rem(y + 1, 4), lax.rem(y + 3, 4)
    twin = device(x, y, z, 1 - core)
    along = [device(x, y, lax.rem(z + d, 8), core) for d in range(1, 8)]
    greeted = (
        along
        + [device(lax.rem(x + d, 4), y, z, core) for d in range(1, 4)]
        + [device(lax.rem(x + d, 4), y1, z, core) for d in range(1, 4)]
        + [device(x, ahead, z, core), device(x, back, z, core)]
        + [device(x, ahead, z, 1 - core), device(x, back, z, 1 - core), twin]
    )
    tops = [pltpu.make_async_copy(prior.at[pl.ds(q * 256, 8)], ends.at[q], quarters.at[q]) for q in range(4)]
    for copy in tops:
        copy.start()
    greet(greeted)
    prepare(ids, offsets, pts, rows, some_rows, z, panel)
    for copy in tops:
        copy.wait()
    for h in range(2):
        own[h * 8 : h * 8 + 8, :] = jnp.concatenate([ends[2 * h, 0:4, :], ends[2 * h + 1, 0:4, :]])
    pl.semaphore_wait(pltpu.get_barrier_semaphore(), len(greeted))
    points = [send(pts, zpts.at[d], psz.at[d], prz.at[d], along[d]) for d in range(7)]
    begin(points)
    prior_ring = Ring(own, pe, sems[:count], 0)
    cover_ring = Ring(some, ce, sems[count : 2 * count], core)
    local_prior = pltpu.make_async_copy(own, pe.at[panel, row], here.at[0])
    local_mine = pltpu.make_async_copy(prior.at[pl.ds(panel * 256, 256)], mine.at[panel], here.at[1])
    local_prior.start()
    local_mine.start()
    begin(prior_ring.z_copies())
    row_terms(some_rows, some_lhs, 2)
    arrive(points)
    total = pts[...]
    for d in range(7):
        total = total + zpts[d]
    cols[base] = total
    spread = [
        send(cols.at[base], cols.at[base], ps.at[d], pr.at[d],
             {"row": lax.rem(base + d + 1, 8) * 8 + z, "panel": panel})
        for d in range(7)
    ]
    begin(spread)

    def start_ring(ring, local):
        local.wait()
        arrive(ring.z_copies())
        begin(ring.middle(), ring.last(0), ring.hand(0, 0))

    row_terms(rows, lhs, 32)
    arrive(spread)
    for t in range(2):
        column_terms(cols, rhs, panel * 2 + t)
    cover_block(some_lhs, rhs, some, 0, 2, panel * 256, 0)
    local_cover = pltpu.make_async_copy(some, ce.at[panel, row], here.at[2])
    local_cover.start()
    begin(cover_ring.z_copies())

    def others(t, _):
        column_terms(cols, rhs, lax.rem(panel * 2 + t, 8))
        return 0

    start_ring(prior_ring, local_prior)
    lax.fori_loop(2, 8, others, 0)

    def exchange():
        first, second, landing = [], [], []
        for w in range(2):
            to = (ahead, back)[w]
            source = (back, ahead)[w] // 2 * 2 + core
            for c in range(2):
                rows = (1 - y // 2) * 512 + c * 256 + w * 128
                first.append(send(prior.at[pl.ds(rows, 128)], relay.at[w, c], qs.at[w, c], qr.at[w, c],
                                  device(x, to, z, core)))
                hop = functools.partial(send, relay.at[w, c], mine.at[source, pl.ds(w * 128, 128)], qs2.at[w, c])
                second.append(hop(qr2.at[w, core], device(x, to, z, c)))
                landing.append(hop(qr2.at[w, c], device(x, to, z, c)))
        rows = (y // 2 * 2 + 1 - core) * 256
        return first, second, landing, [send(prior.at[pl.ds(rows, 256)], mine.at[panel], ts, tr, twin)]

    def middle_in(ring):
        arrive(ring.middle())
        begin(ring.middle_far(), ring.last(1), ring.last(3), ring.hand(1, 0), ring.hand(3, 0))

    def middle_far_in(ring):
        arrive(ring.middle_far())
        begin(ring.last(2), ring.hand(2, 0))

    def last_in(ring, *ks):
        for k in ks:
            arrive(ring.last(k))
            begin(ring.last_far(k), ring.hand(k, 1), ring.hand(k, 3))

    def last_far_in(ring):
        for k in range(4):
            arrive(ring.last_far(k))
            begin(ring.hand(k, 2))

    def exchange_out():
        first, _, _, near = exchange()
        begin(first, near)

    def exchange_on():
        first, second, _, _ = exchange()
        arrive(first)
        begin(second)

    steps = {
        3: lambda: start_ring(cover_ring, local_cover),
        6: lambda: middle_in(prior_ring),
        7: lambda: (middle_in(cover_ring), exchange_out()),
        9: lambda: last_in(prior_ring, 0),
        10: lambda: middle_far_in(prior_ring),
        11: lambda: middle_far_in(cover_ring),
        15: lambda: last_in(prior_ring, 1, 3),
        17: lambda: last_in(cover_ring, 0),
        18: exchange_on,
        20: lambda: last_in(prior_ring, 2),
        21: lambda: last_in(cover_ring, 1, 3),
        23: lambda: last_in(cover_ring, 2),
        27: lambda: last_far_in(prior_ring),
        29: lambda: last_far_in(cover_ring),
    }

    def blocks(i, _):
        for when, step in steps.items():
            pl.when(i == when)(functools.partial(run, step))
        at = lax.rem(i, 4) * 256
        cover_block(lhs, rhs, cover, i // 4, 4, at, at)
        return 0

    lax.fori_loop(0, 32, blocks, 0)
    first, second, landing, near = exchange()
    for ring in (prior_ring, cover_ring):
        for k in range(4):
            for i in range(4):
                arrive(ring.hand(k, i))
    arrive(landing, near)
    local_mine.wait()
    for copy in points + spread + prior_ring.all() + cover_ring.all() + first + second + near:
        copy.wait_send()


def gather(ids, offsets, prior):
    dma = pltpu.SemaphoreType.DMA
    hbm, vmem = pl.BlockSpec(memory_space=pl.ANY), pl.BlockSpec(memory_space=pltpu.VMEM)
    ring = [dma(size) for size in Ring.sizes]
    return pl.pallas_call(
        gather_kernel,
        out_shape=[
            jax.ShapeDtypeStruct((4, 64, 16, 512), f32),
            jax.ShapeDtypeStruct((4, 64, 16, 256), f32),
            jax.ShapeDtypeStruct((4, 256, 512), f32),
            jax.ShapeDtypeStruct((256, B), f32),
        ],
        in_specs=[vmem, vmem, hbm],
        out_specs=[hbm, hbm, hbm, vmem],
        scratch_shapes=[
            pltpu.VMEM((32, 128), f32), pltpu.VMEM((256, 128), f32), pltpu.VMEM((16, 128), f32),
            pltpu.VMEM((4, 8, 512), f32), pltpu.VMEM((16, 512), f32),
            pltpu.VMEM((16, 256), f32), pltpu.VMEM((7, 32, 128), f32), pltpu.VMEM((8, 32, 128), f32),
            pltpu.VMEM((2, 2, 128, 512), f32),
            pltpu.VMEM((4096, TERMS), bf16), pltpu.VMEM((256, TERMS), bf16), pltpu.VMEM((Q, TERMS, B), bf16),
            *ring, *ring, dma((4,)), dma((3,)), dma((7,)), dma((7,)), dma((7,)), dma((7,)),
            dma((2, 2)), dma((2, 2)), dma((2, 2)), dma((2, 2)), dma, dma,
        ],
        compiler_params=pltpu.CompilerParams(
            collective_id=0, has_side_effects=True, vmem_limit_bytes=VMEM_LIMIT
        ),
    )(ids, offsets, prior)


def split(v):
    hi = v.astype(bf16)
    return hi, (v - hi.astype(f32)).astype(bf16)


def dot3(ah, al, bh, bl):
    dot = functools.partial(lax.dot_general, dimension_numbers=NT, preferred_element_type=f32)
    return dot(ah, bh) + (dot(ah, bl) + dot(al, bh))


def factor_inverse(block):
    sub = lax.broadcasted_iota(jnp.int32, (8, 128), 0)
    lane = lax.broadcasted_iota(jnp.int32, (8, 128), 1)
    rest = [block[8 * s : 8 * s + 8, :] for s in range(16)]
    unit = [jnp.where(lane == sub + 8 * s, 1.0, 0.0).astype(f32) for s in range(16)]

    def down(v, k):
        return jnp.broadcast_to(v[k : k + 1, :], (8, 128))

    def across(v, k):
        return jnp.broadcast_to(v[:, k : k + 1], (8, 128))

    out = []
    for s in range(16):
        strip, other = rest[s], unit[s]
        cols = [across(strip, 8 * s + k) for k in range(8)]
        final = jnp.zeros((8, 128), f32)
        for k in range(0, 8, 2):
            upper, lower = sub == k, sub == k + 1
            pair = upper | lower
            p, q, r = down(cols[k], k), down(cols[k + 1], k), down(cols[k + 1], k + 1)
            inverse = 1.0 / (p * r - q * q)
            ip, iq, ir = r * inverse, -(q * inverse), p * inverse
            x, y = cols[k], cols[k + 1]
            cx = jnp.where(upper, -ip, jnp.where(lower, -iq, x * ip + y * iq))
            cy = jnp.where(upper, -iq, jnp.where(lower, -ir, x * iq + y * ir))

            def step(v):
                return jnp.where(pair, 0.0, v) - (cx * down(v, k) + cy * down(v, k + 1))

            root = lax.rsqrt(p)
            ox, oy = down(other, k), down(other, k + 1)
            ratio = q * root * root
            second = (oy - ox * ratio) * lax.rsqrt(r - q * ratio)
            final = jnp.where(upper, ox * root, jnp.where(lower, second, final))
            strip, other = step(strip), step(other)
            for j in range(k + 2, 8):
                cols[j] = step(cols[j])
        out.append(final)
        for t in range(s + 1, 16):
            a, b = rest[t], unit[t]
            for k in range(8):
                c = across(rest[t], 8 * s + k)
                a = a - c * down(strip, k)
                b = b - c * down(other, k)
            rest[t], unit[t] = a, b
    return jnp.concatenate(out, axis=0)


def solve_kernel(every, panel_cover, mine, own_cover, out, raw, raw_mine, ph, lo, m, lh, ll, column, sem):
    row, panel = lax.axis_index("row"), lax.axis_index("panel")
    first = (row * 4 + panel) * 4
    loads = [pltpu.make_async_copy(every.at[p], raw.at[p], sem.at[p]) for p in range(4)]
    load_mine = pltpu.make_async_copy(mine, raw_mine, sem.at[4])
    load_own = pltpu.make_async_copy(own_cover, m.at[pl.ds(1024, 256)], sem.at[5])
    load_cover = [
        pltpu.make_async_copy(
            panel_cover.at[j, pl.ds(j * 256, B - j * 256)],
            m.at[pl.ds(j * 256, B - j * 256), pl.ds(j * 256, 256)],
            sem.at[6 + j],
        )
        for j in range(4)
    ]
    for copy in [*loads, load_mine, load_own, *load_cover]:
        copy.start()
    for p in range(4):
        cp = slice(p * 512, p * 512 + 512)
        loads[p].wait()

        def halves(c, _):
            rc = pl.ds(pl.multiple_of(c * 128, 128), 128)
            ph[rc, cp], lo[rc, cp] = split(raw[p, rc, :])
            return 0

        lax.fori_loop(0, 8, halves, 0)

    load_mine.wait()
    for p in range(4):
        cp = slice(p * 512, p * 512 + 512)
        ph[1024:1280, cp], lo[1024:1280, cp] = split(raw_mine[p])
    load_own.wait()
    for copy in load_cover:
        copy.wait()
    ids = lax.broadcasted_iota(jnp.int32, (256, 256), 0)
    col = lax.broadcasted_iota(jnp.int32, (256, 256), 1)
    unit = jnp.where(ids == col, 1.0, 0.0).astype(f32)
    for j in range(4):
        cj = slice(j * 256, j * 256 + 256)
        own = jnp.where((ids < 4) & (col + j * 256 == first + ids), 1.0, 0.0).astype(f32)
        m[1024:1280, cj] = m[1024:1280, cj] + own
        m[cj, cj] = m[cj, cj] + unit

    def update(j, _):
        cj = pl.ds(pl.multiple_of(j * 256, 256), 256)

        def block(i, _):
            ci = pl.ds(pl.multiple_of(i * 256, 256), 256)
            m[ci, cj] = m[ci, cj] - dot3(ph[ci, :], lo[ci, :], ph[cj, :], lo[cj, :])
            return 0

        lax.fori_loop(j, 5, block, 0)
        return 0

    lax.fori_loop(0, 4, update, 0)

    def left(k):
        ck, before = slice(k * 128, k * 128 + 128), slice(0, k * 128)
        for c in range(k // 2, 5):
            rc = slice(c * 256, c * 256 + 256)
            if k == 0:
                column[rc, :] = m[rc, ck]
            else:
                column[rc, :] = m[rc, ck] - dot3(lh[rc, before], ll[rc, before], lh[ck, before], ll[ck, before])

    def right(k, inverse):
        ck = slice(k * 128, k * 128 + 128)
        ih, il = split(inverse)
        for c in range((k + 1) // 2, 5):
            rc = slice(c * 256, c * 256 + 256)
            rh, rl = split(column[rc, :])
            v = dot3(rh, rl, ih, il)
            if c < 4:
                lh[rc, ck], ll[rc, ck] = split(v)
            else:
                if k < 7:
                    lh[rc, ck], ll[rc, ck] = split(v)
                out[:, ck] = v

    left(0)

    def one(k, _):
        inverse = factor_inverse(column[pl.ds(pl.multiple_of(k * 128, 128), 128), :])

        def finish(kk):
            right(kk, inverse)
            if kk < 7:
                left(kk + 1)

        for kk in range(8):
            pl.when(k == kk)(functools.partial(finish, kk))
        return 0

    lax.fori_loop(0, 8, one, 0)


def solve(every, panel_cover, mine, own_cover):
    vmem = pl.BlockSpec(memory_space=pltpu.VMEM)
    return pl.pallas_call(
        solve_kernel,
        out_shape=jax.ShapeDtypeStruct((256, B), f32),
        in_specs=[pl.BlockSpec(memory_space=pl.ANY)] * 4,
        out_specs=vmem,
        scratch_shapes=[
            pltpu.VMEM((4, B, 512), f32), pltpu.VMEM((4, 256, 512), f32),
            pltpu.VMEM((1280, 2048), bf16), pltpu.VMEM((1280, 2048), bf16),
            pltpu.VMEM((1280, B), f32),
            pltpu.VMEM((1280, B), bf16), pltpu.VMEM((1280, B), bf16),
            pltpu.VMEM((1280, 128), f32), pltpu.SemaphoreType.DMA((10,)),
        ],
        compiler_params=pltpu.CompilerParams(vmem_limit_bytes=VMEM_LIMIT),
    )(every, panel_cover, mine, own_cover)


def local(pixel_ids, quad_offsets, prior_factor):
    every, panel_cover, mine, own_cover = gather(pixel_ids.reshape(1, 1024), quad_offsets, prior_factor)
    return solve(every.reshape(4, B, 512), panel_cover.reshape(4, B, 256), mine, own_cover)


def solution(mesh):
    return jax.shard_map(
        local,
        mesh=mesh,
        in_specs=(P("row"), P(None, None, "row"), P("row", "panel")),
        out_specs=P(("row", "panel"), None),
        check_vma=False,
    )
```
